256 devices in a mesh: section: 8 (over x, core), span: 32 (over y, z).
Axes of the slice: x: 4, y: 4, z: 8, core: 2. Of those that a mesh axis runs over, the one named last changes fastest.
Arguments:
- inverse_blocks: bfloat16 [32, 768, 768], P('section'), may hold values from -1.2 to 1.2
- coupling: float32 [32, 768], P('section'), may hold values from 0.05 to 0.3
- sources: bfloat16 [8, 768, 12288], P('section', None, 'span'), may hold values from -36 to 36
Outputs:
- basis: bfloat16 [8, 768, 12288], P('section', None, 'span')
- upper: float32 [8, 48, 48], P('section')
The draws below stay inside these ranges and needn't reach their ends.
All inputs are finite; a program needn't handle non-finite values.
Results may differ from the reference program's by a relative error of at most 0.03.
Values may be sent and summed in bfloat16 or wider, within the bound.
A program may use at most 64 MiB of HBM per device.

```python
import math
import jax
import jax.numpy as jnp
from jax import lax

K = 48
STATIONS = 4
FN = 768
NZ = 256
STATIONS_ALL = 32
N_SECTION = 8


def draw_inverse_blocks(key, part):
    noise = jax.random.truncated_normal(key, -4.0, 4.0, (STATIONS_ALL, FN, FN), jnp.float32)
    blocks = 0.9 * jnp.eye(FN, dtype=jnp.float32)[None] + 0.45 * noise / jnp.sqrt(float(FN))
    return blocks.astype(jnp.bfloat16)


def draw_sources(key, part):
    key_rows = jax.random.fold_in(key, 11)
    key_base = jax.random.fold_in(key, 12)
    row_scale = jnp.exp(jax.random.uniform(key_rows, (FN,), jnp.float32, jnp.log(0.3), jnp.log(3.0)))
    positions = jnp.arange(NZ, dtype=jnp.float32) / float(max(NZ - 1, 1))
    span_scale = 0.3 * jnp.power(10.0, positions)
    base = jax.random.truncated_normal(key_base, -4.0, 4.0, (N_SECTION, FN, NZ, K), jnp.float32)
    values = base * row_scale[None, :, None, None] * span_scale[None, None, :, None]
    return values.reshape(N_SECTION, FN, NZ * K).astype(jnp.bfloat16)


def block_levels(key, shape, cuts, least, top_value):
    def one(axis_at, shards_of):
        draws = jax.random.uniform(jax.random.fold_in(jax.random.fold_in(key, 6), axis_at), (shards_of,), jnp.float32, least / len(cuts), top_value / len(cuts))
        return jnp.repeat(jnp.exp(draws), shape[axis_at] // shards_of).reshape((-1,) + (1,) * (len(shape) - axis_at - 1))

    factor_of = one(*cuts[0])
    for cut in cuts[1:]:
        factor_of = factor_of * one(*cut)
    return factor_of


def setup_inputs(seed: int = 0) -> dict:
    seeds = jax.random.split(jax.random.key(seed), 4)
    inverse_blocks = draw_inverse_blocks(jax.random.fold_in(seeds[3], 71), 0)
    coupling = jnp.clip(jnp.exp(math.log(0.3) - 1.7917595 * jax.random.uniform(seeds[1], (STATIONS_ALL, FN), jnp.float32) ** block_levels(seeds[1], (STATIONS_ALL, FN), ((0, 8),), -0.2, 0.2)), 0.05, 0.3)
    sources = draw_sources(jax.random.fold_in(seeds[3], 71), 0)
    return dict(inverse_blocks=inverse_blocks, coupling=coupling, sources=sources)


def station_step(state, blocks, rates):
    wide = state.astype(jnp.float32)
    spread = jnp.roll(wide, -1, 1) + jnp.roll(wide, 1, 1) - 2.0 * wide
    update = (wide + rates[:, None, None] * spread).astype(jnp.bfloat16)
    moved = jnp.dot(blocks.astype(jnp.float32), update.reshape(FN, -1).astype(jnp.float32), preferred_element_type=jnp.float32)
    return moved.astype(jnp.bfloat16).reshape(state.shape)

def orthonormalize(state):
    flat_rows = state.reshape(FN * NZ, K)
    summed = jnp.dot(flat_rows.T.astype(jnp.float32), flat_rows.astype(jnp.float32), preferred_element_type=jnp.float32)
    scaled = summed / float(FN * NZ)
    factor = jnp.linalg.cholesky(scaled)
    inverse = jax.scipy.linalg.solve_triangular(factor, jnp.eye(K, dtype=jnp.float32), lower=True)
    basis_rows = jnp.dot(flat_rows.astype(jnp.float32), inverse.T, precision=lax.Precision.HIGHEST)
    return (basis_rows.astype(jnp.bfloat16).reshape(FN, NZ * K), factor.T)

def reference(inverse_blocks, coupling, sources):
    incoming = jnp.zeros((FN, NZ, K), jnp.bfloat16)
    bases = []
    uppers = []
    for group_index in reversed(range(N_SECTION)):
        added = incoming.astype(jnp.float32) + sources[group_index].reshape(FN, NZ, K).astype(jnp.float32)
        state = added.astype(jnp.bfloat16)
        for station in reversed(range(STATIONS)):
            place = group_index * STATIONS + station
            state = station_step(state, inverse_blocks[place], coupling[place])
        incoming = state
        basis_one, upper_one = orthonormalize(state)
        bases.append(basis_one)
        uppers.append(upper_one)
    bases = bases[::-1]
    uppers = uppers[::-1]
    return (jnp.stack(bases), jnp.stack(uppers))
```

```python
import functools

import jax
import jax.numpy as jnp
from jax import lax
from jax.experimental import pallas as pl
from jax.experimental.pallas import tpu as pltpu
from jax.sharding import PartitionSpec as P

MESH = pl.DeviceIdType.MESH
K = 48
STATIONS = 4
KC = 16
CHUNKS = K // KC
BF = jnp.bfloat16
F32 = jnp.float32


def grid_sizes(mesh):
    span = mesh.shape["span"]
    rows = 4 if span == 32 else 2
    return mesh.shape["section"], rows, span // rows


def march_kernel(sizes, lz, fn, a_hbm, c_ref, s_hbm, yt_ref, g_ref,
                 av, at, sv, st, ext, inc, wa, wb, yv, gy, gz,
                 lsem, msend, mrecv, hsend, hrecv, ysend, yrecv, zsend, zrecv):
    ng, ny, nz = sizes
    ns = ny * nz
    rows = lz * KC
    halo = STATIONS * KC
    g = lax.axis_index("section")
    s = lax.axis_index("span")
    my, mz = s // nz, lax.rem(s, nz)
    left = (g, lax.rem(s + ns - 1, ns))
    right = (g, lax.rem(s + 1, ns))
    last = g == ng - 1

    source_copy = pltpu.make_async_copy(s_hbm, sv, lsem.at[STATIONS])
    source_copy.start()
    weight_copies = [pltpu.make_async_copy(a_hbm.at[i], av.at[i], lsem.at[i]) for i in range(STATIONS)]
    for i in reversed(range(STATIONS)):
        weight_copies[i].start()

    barrier = pltpu.get_barrier_semaphore()

    def greet(device):
        pl.semaphore_signal(barrier, inc=1, device_id=device, device_id_type=MESH)

    y_peer = lambda d: (g, lax.rem(my + d, ny) * nz + mz)
    z_peer = lambda d: (g, my * nz + lax.rem(mz + d, nz))
    greet(left)
    greet(right)
    for d in range(1, ny):
        greet(y_peer(d))
    for d in range(1, nz):
        greet(z_peer(d))

    greet((lax.rem(g + ng - 1, ng), s))
    greet((lax.rem(g + 1, ng), s))

    source_copy.wait()
    wide_row = lax.broadcasted_iota(jnp.int32, (rows, lz * K), 0)
    wide_lane = lax.broadcasted_iota(jnp.int32, (rows, lz * K), 1)
    for c in range(CHUNKS):
        pick = (wide_lane == (wide_row // KC) * K + c * KC + lax.rem(wide_row, KC)).astype(F32).astype(BF)
        st[c] = lax.dot_general(pick, sv[...], (((1,), (1,)), ((), ())), preferred_element_type=F32).astype(BF)

    pl.semaphore_wait(barrier, ny + nz + 2)

    def main_copy(c):
        return pltpu.make_async_remote_copy(
            src_ref=yv.at[c], dst_ref=inc.at[c], send_sem=msend.at[c], recv_sem=mrecv.at[c],
            device_id=(lax.rem(g + ng - 1, ng), s), device_id_type=MESH)

    def halo_copy(c, side):
        start, target, device = ((halo, halo + rows, left), (rows, 0, right))[side]
        return pltpu.make_async_remote_copy(
            src_ref=ext.at[c, pl.ds(start, halo)], dst_ref=ext.at[c, pl.ds(target, halo)],
            send_sem=hsend.at[c, side], recv_sem=hrecv.at[c, side],
            device_id=device, device_id_type=MESH)

    @pl.when(last)
    def _():
        for c in range(CHUNKS):
            ext[c, pl.ds(halo, rows), :] = st[c]
            halo_copy(c, 0).start()
            halo_copy(c, 1).start()

    for i in reversed(range(STATIONS)):
        weight_copies[i].wait()
        at[i] = av[i].T

    def prepare(c):
        @pl.when(jnp.logical_not(last))
        def _():
            main_copy(c).wait_recv()
            ext[c, pl.ds(halo, rows), :] = (inc[c].astype(F32) + st[c].astype(F32)).astype(BF)
            halo_copy(c, 0).start()
            halo_copy(c, 1).start()

    def station(index, value, count, store):
        w = value.astype(F32)
        center = w[KC:-KC]
        spread = w[2 * KC:] + w[:-2 * KC] - 2.0 * center
        update = (center + c_ref[index:index + 1, :] * spread).astype(BF)
        store(jnp.dot(update, at[index], preferred_element_type=F32).astype(BF))

    def put(ref, *where):
        def store(v):
            ref[where] = v
        return store

    def compute(c):
        n = rows + 2 * halo
        step = 2 * KC
        halo_copy(c, 0).wait_recv()
        halo_copy(c, 1).wait_recv()
        station(3, ext[c], n - step, put(wa, pl.ds(0, n - step), slice(None)))
        station(2, wa[pl.ds(0, n - step), :], n - 2 * step, put(wb, pl.ds(0, n - 2 * step), slice(None)))
        station(1, wb[pl.ds(0, n - 2 * step), :], n - 3 * step, put(wa, pl.ds(0, n - 3 * step), slice(None)))
        station(0, wa[pl.ds(0, n - 3 * step), :], n - 4 * step, put(yv, c))

        @pl.when(g > 0)
        def _():
            main_copy(c).start()

    prepare(0)

    def chunk_step(c, carry):
        @pl.when(c < CHUNKS - 1)
        def _():
            prepare(c + 1)

        compute(c)
        return carry

    lax.fori_loop(0, CHUNKS, chunk_step, 0)

    total = CHUNKS * rows
    flat = yv[...].reshape(total, fn)
    gram = lax.dot_general(flat, flat, (((1,), (1,)), ((), ())), preferred_element_type=F32)
    z_of_row = lax.rem(lax.broadcasted_iota(jnp.int32, (total, total), 0), rows) // KC
    z_of_lane = lax.rem(lax.broadcasted_iota(jnp.int32, (total, total), 1), rows) // KC
    gram = jnp.where(z_of_row == z_of_lane, gram, 0.0)
    gram = gram.reshape(CHUNKS, lz, KC, total).sum(1).reshape(K, total)
    lane = lax.broadcasted_iota(jnp.int32, (K, rows), 1)
    packed = jnp.zeros((K, rows), F32)
    for c in range(CHUNKS):
        tile = gram[:, c * rows:(c + 1) * rows]
        shift = rows // 2
        while shift >= KC:
            tile = tile + pltpu.roll(tile, shift, 1)
            shift //= 2
        packed = jnp.where(lane // KC == c, tile, packed)

    gy[my] = packed

    def y_copy(d):
        return pltpu.make_async_remote_copy(
            src_ref=gy.at[my], dst_ref=gy.at[my], send_sem=ysend.at[d - 1], recv_sem=yrecv.at[d - 1],
            device_id=y_peer(d), device_id_type=MESH)

    def z_copy(d):
        return pltpu.make_async_remote_copy(
            src_ref=gz.at[mz], dst_ref=gz.at[mz], send_sem=zsend.at[d - 1], recv_sem=zrecv.at[d - 1],
            device_id=z_peer(d), device_id_type=MESH)

    for d in range(1, ny):
        y_copy(d).start()
    yt_ref[...] = flat.T
    for d in range(1, ny):
        y_copy(d).wait_recv()
    acc = gy[0]
    for i in range(1, ny):
        acc = acc + gy[i]
    gz[mz] = acc
    for d in range(1, nz):
        z_copy(d).start()
    for d in range(1, nz):
        z_copy(d).wait_recv()
    acc = gz[0]
    for i in range(1, nz):
        acc = acc + gz[i]
    g_ref[...] = acc

    for c in range(CHUNKS):
        halo_copy(c, 0).wait_send()
        halo_copy(c, 1).wait_send()

        @pl.when(g > 0)
        def _():
            main_copy(c).wait_send()

    for d in range(1, ny):
        y_copy(d).wait_send()
    for d in range(1, nz):
        z_copy(d).wait_send()


def basis_kernel(lz, count, yt_ref, g_ref, o_ref, u_ref):
    rows = lz * KC
    lane = lax.broadcasted_iota(jnp.int32, (K, 128), 1)
    row = lax.broadcasted_iota(jnp.int32, (K, 128), 0)
    scaled = g_ref[...] * (1.0 / count)
    w = jnp.where(lane < K, scaled, jnp.where(lane == row + 64, 1.0, 0.0))
    for j in range(K):
        pivot = w[j:j + 1, :]
        inv = lax.rsqrt(w[j:j + 1, j:j + 1])
        unit = pivot * inv
        column = w[:, j:j + 1] * inv
        w = jnp.where(row == j, unit, w - jnp.where(row > j, column, 0.0) * unit)
    u_ref[...] = jnp.where(lane >= row, w, 0.0)[:, :K]
    tile_row = lax.broadcasted_iota(jnp.int32, (K, lz * K), 0)
    tile_lane = lax.broadcasted_iota(jnp.int32, (K, lz * K), 1)
    spread = (tile_row == lax.rem(tile_lane, K)).astype(F32).astype(BF)
    high = w.astype(BF)
    low = (w - high.astype(F32)).astype(BF)
    block_row = lax.broadcasted_iota(jnp.int32, (rows, lz * K), 0)
    block_lane = lax.broadcasted_iota(jnp.int32, (rows, lz * K), 1)
    same = block_row // KC == block_lane // K
    out = None
    for part in (high, low):
        tiled = lax.dot_general(part, spread, (((0,), (0,)), ((), ())), preferred_element_type=F32)
        blocks = []
        for c in range(CHUNKS):
            one = tiled[64 + c * KC:64 + (c + 1) * KC]
            blocks.append(jnp.where(same, jnp.concatenate([one] * lz, axis=0), 0.0))
        block = jnp.concatenate(blocks, axis=0).astype(BF)
        term = jnp.dot(yt_ref[...], block, preferred_element_type=F32)
        out = term if out is None else out + term
    o_ref[...] = out.astype(BF)


def local(sizes, count, inverse_blocks, coupling, sources):
    ng, ny, nz = sizes
    fn = inverse_blocks.shape[1]
    lz = sources.shape[2] // K
    rows = lz * KC
    halo = STATIONS * KC
    n = rows + 2 * halo
    hbm = pl.BlockSpec(memory_space=pl.ANY)
    vmem = pl.BlockSpec(memory_space=pltpu.VMEM)
    dma = pltpu.SemaphoreType.DMA
    yt, gram = pl.pallas_call(
        functools.partial(march_kernel, sizes, lz, fn),
        name="march",
        out_shape=(jax.ShapeDtypeStruct((fn, CHUNKS * rows), BF), jax.ShapeDtypeStruct((K, 128), F32)),
        in_specs=[hbm, vmem, hbm],
        out_specs=(vmem, vmem),
        scratch_shapes=[
            pltpu.VMEM((STATIONS, fn, fn), BF),
            pltpu.VMEM((STATIONS, fn, fn), BF),
            pltpu.VMEM((fn, lz * K), BF),
            pltpu.VMEM((CHUNKS, rows, fn), BF),
            pltpu.VMEM((CHUNKS, n, fn), BF),
            pltpu.VMEM((CHUNKS, rows, fn), BF),
            pltpu.VMEM((n, fn), BF),
            pltpu.VMEM((n, fn), BF),
            pltpu.VMEM((CHUNKS, rows, fn), BF),
            pltpu.VMEM((ny, K, 128), F32),
            pltpu.VMEM((nz, K, 128), F32),
            dma((STATIONS + 1,)),
            dma((CHUNKS,)),
            dma((CHUNKS,)),
            dma((CHUNKS, 2)),
            dma((CHUNKS, 2)),
            dma((ny - 1,)),
            dma((ny - 1,)),
            dma((nz - 1,)),
            dma((nz - 1,)),
        ],
        compiler_params=pltpu.CompilerParams(collective_id=0, has_side_effects=True, vmem_limit_bytes=48 << 20),
    )(inverse_blocks, coupling, sources[0])
    basis, upper = pl.pallas_call(
        functools.partial(basis_kernel, lz, count),
        name="basis",
        out_shape=(jax.ShapeDtypeStruct((fn, lz * K), BF), jax.ShapeDtypeStruct((K, K), F32)),
        in_specs=[vmem, vmem],
        out_specs=(vmem, vmem),
        compiler_params=pltpu.CompilerParams(vmem_limit_bytes=48 << 20),
    )(yt, gram)
    return basis[None], upper[None]


def solution(mesh):
    placed = (P("section", None, None), P("section", None), P("section", None, "span"))
    sizes = grid_sizes(mesh)

    def whole(inverse_blocks, coupling, sources):
        count = float(sources.shape[1] * sources.shape[2] // K)
        return jax.shard_map(
            functools.partial(local, sizes, count),
            mesh=mesh,
            in_specs=placed,
            out_specs=(P("section", None, "span"), P("section", None, None)),
            check_vma=False,
        )(inverse_blocks, coupling, sources)

    return whole
```

```python
import functools

import jax
import jax.numpy as jnp
from jax import lax
from jax.experimental import pallas as pl
from jax.experimental.pallas import tpu as pltpu
from jax.sharding import PartitionSpec as P

MESH = pl.DeviceIdType.MESH
K = 48
STATIONS = 4
KC = 8
CHUNKS = 3
BF = jnp.bfloat16
F32 = jnp.float32


def grid_sizes(mesh):
    span = mesh.shape["span"]
    rows = 4 if span == 32 else 2
    return mesh.shape["section"], rows, span // rows


def march_kernel(sizes, lz, fn, a_hbm, c_hbm, s_hbm, yt_ref, g_ref,
                 av, at, cv, cc, sv, tmp, sa, sb, ext, inc, wa, wb, ym, yf, gy, gz,
                 lsem, wsend, wrecv, csend, crecv, ssend, srecv, bsend, brecv,
                 msend, mrecv, hsend, hrecv, xsend, xrecv, ysend, yrecv, zsend, zrecv):
    ng, ny, nz = sizes
    ns = ny * nz
    rows = lz * KC
    half = STATIONS * KC
    g = lax.axis_index("section")
    s = lax.axis_index("span")
    core = lax.rem(g, 2)
    my, mz = s // nz, lax.rem(s, nz)
    left = (g, lax.rem(s + ns - 1, ns))
    right = (g, lax.rem(s + 1, ns))
    other = (g + 1 - 2 * core, s)
    below = (lax.rem(g + ng - 2, ng), s)
    above = (lax.rem(g + 2, ng), s)
    first_chip = g >= ng - 2
    last_chip = g < 2
    is_one = core == 1
    is_zero = core == 0

    source_copy = pltpu.make_async_copy(s_hbm, sv, lsem.at[STATIONS])
    source_copy.start()
    rate_copy = pltpu.make_async_copy(c_hbm, cv, lsem.at[STATIONS + 1])
    rate_copy.start()
    weight_copies = [pltpu.make_async_copy(a_hbm.at[i], av.at[i], lsem.at[i]) for i in range(STATIONS)]
    for i in reversed(range(STATIONS)):
        weight_copies[i].start()

    barrier = pltpu.get_barrier_semaphore()

    def greet(device):
        pl.semaphore_signal(barrier, inc=1, device_id=device, device_id_type=MESH)

    y_peer = lambda d: (g, lax.rem(my + d, ny) * nz + mz)
    z_peer = lambda d: (g, my * nz + lax.rem(mz + d, nz))
    for device in [left, right, other, below, above]:
        greet(device)
    for d in range(1, ny):
        greet(y_peer(d))
    for d in range(1, nz):
        greet(z_peer(d))

    def remote(src, dst, send, recv, device):
        return pltpu.make_async_remote_copy(
            src_ref=src, dst_ref=dst, send_sem=send, recv_sem=recv, device_id=device, device_id_type=MESH)

    weight_cross = lambda p, i: remote(at.at[p, i], at.at[p, i], wsend.at[i], wrecv.at[i], other)
    rate_cross = lambda p: remote(cc.at[p], cc.at[p], csend.at[0], crecv.at[0], other)
    middle = pl.ds(half, rows)
    source_cross_a = lambda j: remote(tmp.at[j], sa.at[j], ssend.at[j], srecv.at[j], other)
    source_cross_b = lambda j: remote(tmp.at[j], sb.at[j, middle], ssend.at[j], srecv.at[j], other)
    main_copy = lambda j: remote(ym.at[0, j], inc.at[j], msend.at[j], mrecv.at[j], below)
    cross_y = lambda j: remote(ym.at[1 - core, j], yf.at[core, j], xsend.at[j], xrecv.at[j], other)

    def halo_copy(j, side):
        target, device = ((2 * rows, left), (0, right))[side]
        return remote(ext.at[j, pl.ds(rows, rows)], ext.at[j, pl.ds(target, rows)],
                      hsend.at[j, side], hrecv.at[j, side], device)

    def source_halo(j, side):
        start, target, device = ((half, half + rows, left), (rows, 0, right))[side]
        return remote(sb.at[j, pl.ds(start, half)], sb.at[j, pl.ds(target, half)],
                      bsend.at[j, side], brecv.at[j, side], device)

    source_copy.wait()
    wide_row = lax.broadcasted_iota(jnp.int32, (rows, lz * K), 0)
    wide_lane = lax.broadcasted_iota(jnp.int32, (rows, lz * K), 1)
    base_lane = (wide_row // KC) * K + lax.rem(wide_row, KC)

    def columns(h, j):
        pick = (wide_lane == base_lane + (h * (K // 2) + j * KC)).astype(F32).astype(BF)
        return lax.dot_general(pick, sv[...], (((1,), (1,)), ((), ())), preferred_element_type=F32).astype(BF)

    for j in range(CHUNKS):
        tmp[j] = columns(1 - core, j)
        mine = columns(core, j)

        @pl.when(is_one)
        def _():
            sa[j] = mine

        @pl.when(is_zero)
        def _():
            sb[j, middle, :] = mine

    rate_copy.wait()
    cc[core] = jnp.concatenate([cv[...], jnp.zeros_like(cv)], axis=0)
    pl.semaphore_wait(barrier, ny + nz + 3)

    for j in range(CHUNKS):
        @pl.when(is_one)
        def _():
            source_cross_a(j).start()

        @pl.when(is_zero)
        def _():
            source_cross_b(j).start()

    rate_cross(core).start()

    @pl.when(first_chip)
    def _():
        for j in range(CHUNKS):
            @pl.when(is_zero)
            def _():
                source_cross_a(j).wait_recv()

            ext[j, pl.ds(rows, rows), :] = sa[j]
            halo_copy(j, 0).start()
            halo_copy(j, 1).start()

    for i in reversed(range(STATIONS)):
        weight_copies[i].wait()
        at[core, i] = av[i].T
        weight_cross(core, i).start()

    for j in range(CHUNKS):
        @pl.when(is_one)
        def _():
            source_cross_b(j).wait_recv()

        @pl.when(jnp.logical_and(is_zero, jnp.logical_not(first_chip)))
        def _():
            source_cross_a(j).wait_recv()

        source_halo(j, 0).start()
        source_halo(j, 1).start()

    rate_cross(1 - core).wait_recv()

    def prepare(j):
        @pl.when(jnp.logical_not(first_chip))
        def _():
            main_copy(j).wait_recv()
            ext[j, pl.ds(rows, rows), :] = (inc[j].astype(F32) + sa[j].astype(F32)).astype(BF)
            halo_copy(j, 0).start()
            halo_copy(j, 1).start()

    def station(j, p, i, value):
        @pl.when(jnp.logical_and(j == 0, core != p))
        def _():
            weight_cross(p, i).wait_recv()

        w = value.astype(F32)
        center = w[KC:-KC]
        spread = w[2 * KC:] + w[:-2 * KC] - 2.0 * center
        update = (center + cc[p, i:i + 1, :] * spread).astype(BF)
        return jnp.dot(update, at[p, i], preferred_element_type=F32).astype(BF)

    def compute(j):
        n = 3 * rows
        step = 2 * KC
        halo_copy(j, 0).wait_recv()
        halo_copy(j, 1).wait_recv()
        wa[pl.ds(0, n - step), :] = station(j, 1, 3, ext[j])
        wb[pl.ds(0, n - 2 * step), :] = station(j, 1, 2, wa[pl.ds(0, n - step), :])
        wa[pl.ds(0, n - 3 * step), :] = station(j, 1, 1, wb[pl.ds(0, n - 2 * step), :])
        n = 2 * rows
        upper_out = station(j, 1, 0, wa[pl.ds(0, n + step), :])
        wb[pl.ds(0, n), :] = upper_out
        ym[1, j] = wb[middle, :]

        @pl.when(is_one)
        def _():
            yf[1, j] = ym[1, j]

        @pl.when(is_zero)
        def _():
            cross_y(j).start()

        source_halo(j, 0).wait_recv()
        source_halo(j, 1).wait_recv()
        value = (upper_out.astype(F32) + sb[j].astype(F32)).astype(BF)
        wa[pl.ds(0, n - step), :] = station(j, 0, 3, value)
        wb[pl.ds(0, n - 2 * step), :] = station(j, 0, 2, wa[pl.ds(0, n - step), :])
        wa[pl.ds(0, n - 3 * step), :] = station(j, 0, 1, wb[pl.ds(0, n - 2 * step), :])
        ym[0, j] = station(j, 0, 0, wa[pl.ds(0, n - 3 * step), :])

        @pl.when(jnp.logical_not(last_chip))
        def _():
            main_copy(j).start()

        @pl.when(is_zero)
        def _():
            yf[0, j] = ym[0, j]

        @pl.when(is_one)
        def _():
            cross_y(j).start()

    prepare(0)

    def chunk_step(j, carry):
        @pl.when(j < CHUNKS - 1)
        def _():
            prepare(j + 1)

        compute(j)
        return carry

    lax.fori_loop(0, CHUNKS, chunk_step, 0)
    for j in range(CHUNKS):
        cross_y(j).wait_recv()

    total = 2 * CHUNKS * rows
    flat = yf[...].reshape(total, fn)
    gram = lax.dot_general(flat, flat, (((1,), (1,)), ((), ())), preferred_element_type=F32)
    z_of_row = lax.rem(lax.broadcasted_iota(jnp.int32, (total, total), 0), rows) // KC
    z_of_lane = lax.rem(lax.broadcasted_iota(jnp.int32, (total, total), 1), rows) // KC
    gram = jnp.where(z_of_row == z_of_lane, gram, 0.0)
    gram = gram.reshape(2 * CHUNKS, lz, KC, total).sum(1).reshape(K, total)
    lane = lax.broadcasted_iota(jnp.int32, (K, 128), 1)
    packed = jnp.zeros((K, 128), F32)
    for c in range(2 * CHUNKS):
        pair = gram[:, (c // 2) * 128:(c // 2 + 1) * 128]
        tile = jnp.where(lane // rows == c % 2, pair, 0.0)
        for shift in (64, 32, 16, 8):
            tile = tile + pltpu.roll(tile, shift, 1)
        packed = jnp.where(lane // KC == c, tile, packed)
    gy[my] = packed[:K // 2] + pltpu.roll(packed[K // 2:], 64, 1)

    y_copy = lambda d: remote(gy.at[my], gy.at[my], ysend.at[d - 1], yrecv.at[d - 1], y_peer(d))
    z_copy = lambda d: remote(gz.at[mz], gz.at[mz], zsend.at[d - 1], zrecv.at[d - 1], z_peer(d))

    for d in range(1, ny):
        y_copy(d).start()
    yt_ref[...] = flat.T
    for d in range(1, ny):
        y_copy(d).wait_recv()
    acc = gy[0]
    for i in range(1, ny):
        acc = acc + gy[i]
    gz[mz] = acc
    for d in range(1, nz):
        z_copy(d).start()
    for d in range(1, nz):
        z_copy(d).wait_recv()
    acc = gz[0]
    for i in range(1, nz):
        acc = acc + gz[i]
    g_ref[...] = acc

    rate_cross(core).wait_send()
    for i in range(STATIONS):
        weight_cross(core, i).wait_send()
    for j in range(CHUNKS):
        source_cross_a(j).wait_send()
        for side in (0, 1):
            halo_copy(j, side).wait_send()
            source_halo(j, side).wait_send()
        cross_y(j).wait_send()

        @pl.when(jnp.logical_not(last_chip))
        def _():
            main_copy(j).wait_send()

    for d in range(1, ny):
        y_copy(d).wait_send()
    for d in range(1, nz):
        z_copy(d).wait_send()


def basis_kernel(lz, count, yt_ref, g_ref, o_ref, u_ref):
    rows = lz * KC
    lane = lax.broadcasted_iota(jnp.int32, (K, 128), 1)
    row = lax.broadcasted_iota(jnp.int32, (K, 128), 0)
    gram = jnp.concatenate([g_ref[...], pltpu.roll(g_ref[...], 64, 1)], axis=0)
    scaled = gram * (1.0 / count)
    w = jnp.where(lane < K, scaled, jnp.where(lane == row + 64, 1.0, 0.0))
    for j in range(K):
        pivot = w[j:j + 1, :]
        inv = lax.rsqrt(w[j:j + 1, j:j + 1])
        unit = pivot * inv
        column = w[:, j:j + 1] * inv
        w = jnp.where(row == j, unit, w - jnp.where(row > j, column, 0.0) * unit)
    u_ref[...] = jnp.where(lane >= row, w, 0.0)[:, :K]
    tile_row = lax.broadcasted_iota(jnp.int32, (K, lz * K), 0)
    tile_lane = lax.broadcasted_iota(jnp.int32, (K, lz * K), 1)
    spread = (tile_row == lax.rem(tile_lane, K)).astype(F32).astype(BF)
    high = w.astype(BF)
    low = (w - high.astype(F32)).astype(BF)
    block_row = lax.broadcasted_iota(jnp.int32, (rows, lz * K), 0)
    block_lane = lax.broadcasted_iota(jnp.int32, (rows, lz * K), 1)
    same = block_row // KC == block_lane // K
    out = None
    for part in (high, low):
        tiled = lax.dot_general(part, spread, (((0,), (0,)), ((), ())), preferred_element_type=F32)
        blocks = []
        for c in range(2 * CHUNKS):
            one = tiled[64 + c * KC:64 + (c + 1) * KC]
            blocks.append(jnp.where(same, jnp.concatenate([one] * lz, axis=0), 0.0))
        block = jnp.concatenate(blocks, axis=0).astype(BF)
        term = jnp.dot(yt_ref[...], block, preferred_element_type=F32)
        out = term if out is None else out + term
    o_ref[...] = out.astype(BF)


def local(sizes, count, inverse_blocks, coupling, sources):
    ng, ny, nz = sizes
    fn = inverse_blocks.shape[1]
    lz = sources.shape[2] // K
    rows = lz * KC
    half = STATIONS * KC
    hbm = pl.BlockSpec(memory_space=pltpu.HBM)
    vmem = pl.BlockSpec(memory_space=pltpu.VMEM)
    dma = pltpu.SemaphoreType.DMA
    yt, gram = pl.pallas_call(
        functools.partial(march_kernel, sizes, lz, fn),
        name="march",
        out_shape=(jax.ShapeDtypeStruct((fn, lz * K), BF), jax.ShapeDtypeStruct((K // 2, 128), F32)),
        in_specs=[hbm, hbm, hbm],
        out_specs=(vmem, vmem),
        scratch_shapes=[
            pltpu.VMEM((STATIONS, fn, fn), BF),
            pltpu.VMEM((2, STATIONS, fn, fn), BF),
            pltpu.VMEM((STATIONS, fn), F32),
            pltpu.VMEM((2, 2 * STATIONS, fn), F32),
            pltpu.VMEM((fn, lz * K), BF),
            pltpu.VMEM((CHUNKS, rows, fn), BF),
            pltpu.VMEM((CHUNKS, rows, fn), BF),
            pltpu.VMEM((CHUNKS, 2 * half + rows, fn), BF),
            pltpu.VMEM((CHUNKS, 3 * rows, fn), BF),
            pltpu.VMEM((CHUNKS, rows, fn), BF),
            pltpu.VMEM((3 * rows, fn), BF),
            pltpu.VMEM((3 * rows, fn), BF),
            pltpu.VMEM((2, CHUNKS, rows, fn), BF),
            pltpu.VMEM((2, CHUNKS, rows, fn), BF),
            pltpu.VMEM((ny, K // 2, 128), F32),
            pltpu.VMEM((nz, K // 2, 128), F32),
            dma((STATIONS + 2,)),
            dma((STATIONS,)), dma((STATIONS,)),
            dma((1,)), dma((1,)),
            dma((CHUNKS,)), dma((CHUNKS,)),
            dma((CHUNKS, 2)), dma((CHUNKS, 2)),
            dma((CHUNKS,)), dma((CHUNKS,)),
            dma((CHUNKS, 2)), dma((CHUNKS, 2)),
            dma((CHUNKS,)), dma((CHUNKS,)),
            dma((ny - 1,)), dma((ny - 1,)),
            dma((nz - 1,)), dma((nz - 1,)),
        ],
        compiler_params=pltpu.CompilerParams(collective_id=0, has_side_effects=True, vmem_limit_bytes=60 << 20),
    )(inverse_blocks, coupling, sources[0])
    basis, upper = pl.pallas_call(
        functools.partial(basis_kernel, lz, count),
        name="basis",
        out_shape=(jax.ShapeDtypeStruct((fn, lz * K), BF), jax.ShapeDtypeStruct((K, K), F32)),
        in_specs=[vmem, vmem],
        out_specs=(vmem, vmem),
        compiler_params=pltpu.CompilerParams(vmem_limit_bytes=48 << 20),
    )(yt, gram)
    return basis[None], upper[None]


def solution(mesh):
    placed = (P("section", None, None), P("section", None), P("section", None, "span"))
    sizes = grid_sizes(mesh)

    def whole(inverse_blocks, coupling, sources):
        count = float(sources.shape[1] * sources.shape[2] // K)
        return jax.shard_map(
            functools.partial(local, sizes, count),
            mesh=mesh,
            in_specs=placed,
            out_specs=(P("section", None, "span"), P("section", None, None)),
            check_vma=False,
        )(inverse_blocks, coupling, sources)

    return whole
```

```python
import functools

import jax
import jax.numpy as jnp
from jax import lax
from jax.experimental import pallas as pl
from jax.experimental.pallas import tpu as pltpu
from jax.sharding import PartitionSpec as P

MESH = pl.DeviceIdType.MESH
K = 48
STATIONS = 4
KC = 8
CHUNKS = 3
PIECES = 3
BLOCK = 8
BF = jnp.bfloat16
F32 = jnp.float32


def grid_sizes(mesh):
    span = mesh.shape["span"]
    rows = 4 if span == 32 else 2
    return mesh.shape["section"], rows, span // rows


def march_kernel(sizes, lz, fn, count, a_hbm, c_hbm, s_hbm, yt, w_ref,
                 av, at, cv, cc, sv, tmp, sa, sb, ext, inc, wa, wb, ym, yf, gy, gz,
                 lsem, wsend, wrecv, csend, crecv, ssend, srecv, bsend, brecv,
                 msend, mrecv, hsend, hrecv, xsend, xrecv, ysend, yrecv, zsend, zrecv):
    ng, ny, nz = sizes
    ns = ny * nz
    rows = lz * KC
    half = STATIONS * KC
    g = lax.axis_index("section")
    s = lax.axis_index("span")
    core = lax.rem(g, 2)
    my, mz = s // nz, lax.rem(s, nz)
    left = (g, lax.rem(s + ns - 1, ns))
    right = (g, lax.rem(s + 1, ns))
    other = (g + 1 - 2 * core, s)
    below = (lax.rem(g + ng - 2, ng), s)
    above = (lax.rem(g + 2, ng), s)
    first_chip = g >= ng - 2
    last_chip = g < 2
    is_one = core == 1
    is_zero = core == 0

    source_copy = pltpu.make_async_copy(s_hbm, sv, lsem.at[STATIONS])
    source_copy.start()
    rate_copy = pltpu.make_async_copy(c_hbm, cv, lsem.at[STATIONS + 1])
    rate_copy.start()
    weight_copies = [pltpu.make_async_copy(a_hbm.at[i], av.at[i], lsem.at[i]) for i in range(STATIONS)]
    for i in reversed(range(STATIONS)):
        weight_copies[i].start()

    barrier = pltpu.get_barrier_semaphore()

    def greet(device):
        pl.semaphore_signal(barrier, inc=1, device_id=device, device_id_type=MESH)

    y_peer = lambda d: (g, lax.rem(my + d, ny) * nz + mz)
    z_peer = lambda d: (g, my * nz + lax.rem(mz + d, nz))
    for device in [left, right, other, below, above]:
        greet(device)
    for d in range(1, ny):
        greet(y_peer(d))
    for d in range(1, nz):
        greet(z_peer(d))

    def remote(src, dst, send, recv, device):
        return pltpu.make_async_remote_copy(
            src_ref=src, dst_ref=dst, send_sem=send, recv_sem=recv, device_id=device, device_id_type=MESH)

    weight_cross = lambda p, i: remote(at.at[p, i], at.at[p, i], wsend.at[i], wrecv.at[i], other)
    rate_cross = lambda p: remote(cc.at[p], cc.at[p], csend.at[0], crecv.at[0], other)
    middle = pl.ds(half, rows)
    source_cross_a = lambda j: remote(tmp.at[j], sa.at[j], ssend.at[j], srecv.at[j], other)
    source_cross_b = lambda j: remote(tmp.at[j], sb.at[j, middle], ssend.at[j], srecv.at[j], other)
    width = fn // PIECES
    lanes = lambda p: pl.ds(p * width, width)
    everything = pl.ds(0, rows)

    def main_copy(j, p):
        return remote(ym.at[0, j, everything, lanes(p)], inc.at[j, everything, lanes(p)],
                      msend.at[j, p], mrecv.at[j, p], below)

    cross_y = lambda j: remote(ym.at[1 - core, j], yf.at[core, j], xsend.at[j], xrecv.at[j], other)

    def halo_copy(j, side, p):
        target, device = ((2 * rows, left), (0, right))[side]
        return remote(ext.at[j, pl.ds(rows, rows), lanes(p)], ext.at[j, pl.ds(target, rows), lanes(p)],
                      hsend.at[j, side, p], hrecv.at[j, side, p], device)

    def source_halo(j, side):
        start, target, device = ((half, half + rows, left), (rows, 0, right))[side]
        return remote(sb.at[j, pl.ds(start, half)], sb.at[j, pl.ds(target, half)],
                      bsend.at[j, side], brecv.at[j, side], device)

    source_copy.wait()
    total = 2 * CHUNKS * rows
    pick_row = lax.broadcasted_iota(jnp.int32, (total, lz * K), 0)
    pick_lane = lax.broadcasted_iota(jnp.int32, (total, lz * K), 1)
    in_half = lax.rem(pick_row, CHUNKS * rows)
    owner = jnp.where(pick_row < CHUNKS * rows, core, 1 - core)
    in_chunk = lax.rem(in_half, rows)
    source_lane = (in_chunk // KC) * K + owner * (K // 2) + (in_half // rows) * KC + lax.rem(in_chunk, KC)
    pick = (pick_lane == source_lane).astype(F32).astype(BF)
    moved = lax.dot_general(pick, sv[...], (((1,), (1,)), ((), ())), preferred_element_type=F32).astype(BF)
    mine = moved[:CHUNKS * rows].reshape(CHUNKS, rows, fn)
    tmp[...] = moved[CHUNKS * rows:].reshape(CHUNKS, rows, fn)

    @pl.when(is_one)
    def _():
        sa[...] = mine

    @pl.when(is_zero)
    def _():
        sb[:, middle, :] = mine

    rate_copy.wait()
    cc[core] = jnp.concatenate([cv[...], jnp.zeros_like(cv)], axis=0)
    pl.semaphore_wait(barrier, ny + nz + 3)

    for j in range(CHUNKS):
        @pl.when(is_one)
        def _():
            source_cross_a(j).start()

        @pl.when(is_zero)
        def _():
            source_cross_b(j).start()

    rate_cross(core).start()

    @pl.when(first_chip)
    def _():
        for j in range(CHUNKS):
            @pl.when(is_zero)
            def _():
                source_cross_a(j).wait_recv()

            ext[j, pl.ds(rows, rows), :] = sa[j]
            for p in range(PIECES):
                halo_copy(j, 0, p).start()
                halo_copy(j, 1, p).start()

    for i in reversed(range(STATIONS)):
        weight_copies[i].wait()
        at[core, i] = av[i].T
        weight_cross(core, i).start()

    for j in range(CHUNKS):
        @pl.when(is_one)
        def _():
            source_cross_b(j).wait_recv()

        @pl.when(jnp.logical_and(is_zero, jnp.logical_not(first_chip)))
        def _():
            source_cross_a(j).wait_recv()

        source_halo(j, 0).start()
        source_halo(j, 1).start()

    rate_cross(1 - core).wait_recv()

    def prepare(j):
        @pl.when(jnp.logical_not(first_chip))
        def _():
            for p in range(PIECES):
                main_copy(j, p).wait_recv()
                at_piece = (j, everything, lanes(p))
                ext[j, pl.ds(rows, rows), lanes(p)] = (inc[at_piece].astype(F32) + sa[at_piece].astype(F32)).astype(BF)
                halo_copy(j, 0, p).start()
                halo_copy(j, 1, p).start()

    def diffuse(j, p, i, value):
        @pl.when(jnp.logical_and(j == 0, core != p))
        def _():
            weight_cross(p, i).wait_recv()

        w = value.astype(F32)
        center = w[KC:-KC]
        spread = w[2 * KC:] + w[:-2 * KC] - 2.0 * center
        return (center + cc[p, i:i + 1, :] * spread).astype(BF)

    def station(j, p, i, value):
        return jnp.dot(diffuse(j, p, i, value), at[p, i], preferred_element_type=F32).astype(BF)

    def compute(j):
        n = 3 * rows
        step = 2 * KC
        for p in range(PIECES):
            halo_copy(j, 0, p).wait_recv()
            halo_copy(j, 1, p).wait_recv()
        wa[pl.ds(0, n - step), :] = station(j, 1, 3, ext[j])
        wb[pl.ds(0, n - 2 * step), :] = station(j, 1, 2, wa[pl.ds(0, n - step), :])
        wa[pl.ds(0, n - 3 * step), :] = station(j, 1, 1, wb[pl.ds(0, n - 2 * step), :])
        n = 2 * rows
        upper_out = station(j, 1, 0, wa[pl.ds(0, n + step), :])
        wb[pl.ds(0, n), :] = upper_out
        ym[1, j] = wb[middle, :]

        @pl.when(is_one)
        def _():
            yf[1, j] = ym[1, j]

        @pl.when(is_zero)
        def _():
            cross_y(j).start()

        source_halo(j, 0).wait_recv()
        source_halo(j, 1).wait_recv()
        value = (upper_out.astype(F32) + sb[j].astype(F32)).astype(BF)
        wa[pl.ds(0, n - step), :] = station(j, 0, 3, value)
        wb[pl.ds(0, n - 2 * step), :] = station(j, 0, 2, wa[pl.ds(0, n - step), :])
        wa[pl.ds(0, n - 3 * step), :] = station(j, 0, 1, wb[pl.ds(0, n - 2 * step), :])
        update = diffuse(j, 0, 0, wa[pl.ds(0, n - 3 * step), :])
        for p in range(PIECES):
            ym[0, j, everything, lanes(p)] = jnp.dot(
                update, at[0, 0, :, lanes(p)], preferred_element_type=F32).astype(BF)

            @pl.when(jnp.logical_not(last_chip))
            def _():
                main_copy(j, p).start()

        @pl.when(is_zero)
        def _():
            yf[0, j] = ym[0, j]

        @pl.when(is_one)
        def _():
            cross_y(j).start()

    prepare(0)

    def chunk_step(j, carry):
        @pl.when(j < CHUNKS - 1)
        def _():
            prepare(j + 1)

        compute(j)
        return carry

    lax.fori_loop(0, CHUNKS, chunk_step, 0)
    for j in range(CHUNKS):
        cross_y(j).wait_recv()

    flat = yf[...].reshape(total, fn)
    gram = lax.dot_general(flat, flat, (((1,), (1,)), ((), ())), preferred_element_type=F32)
    z_of_row = lax.rem(lax.broadcasted_iota(jnp.int32, (total, total), 0), rows) // KC
    z_of_lane = lax.rem(lax.broadcasted_iota(jnp.int32, (total, total), 1), rows) // KC
    gram = jnp.where(z_of_row == z_of_lane, gram, 0.0)
    gram = gram.reshape(2 * CHUNKS, lz, KC, total).sum(1).reshape(K, total)
    lane = lax.broadcasted_iota(jnp.int32, (K, 128), 1)
    packed = jnp.zeros((K, 128), F32)
    for c in range(2 * CHUNKS):
        pair = gram[:, (c // 2) * 128:(c // 2 + 1) * 128]
        tile = jnp.where(lane // rows == c % 2, pair, 0.0)
        for shift in (64, 32, 16, 8):
            tile = tile + pltpu.roll(tile, shift, 1)
        packed = jnp.where(lane // KC == c, tile, packed)
    gy[my] = packed[:K // 2] + pltpu.roll(packed[K // 2:], 64, 1)

    y_copy = lambda d: remote(gy.at[my], gy.at[my], ysend.at[d - 1], yrecv.at[d - 1], y_peer(d))
    z_copy = lambda d: remote(gz.at[mz], gz.at[mz], zsend.at[d - 1], zrecv.at[d - 1], z_peer(d))

    for d in range(1, ny):
        y_copy(d).start()
    yt[...] = flat.T
    for d in range(1, ny):
        y_copy(d).wait_recv()
    acc = gy[0]
    for i in range(1, ny):
        acc = acc + gy[i]
    gz[mz] = acc
    for d in range(1, nz):
        z_copy(d).start()
    for d in range(1, nz):
        z_copy(d).wait_recv()
    acc = gz[0]
    for i in range(1, nz):
        acc = acc + gz[i]

    rate_cross(core).wait_send()
    for i in range(STATIONS):
        weight_cross(core, i).wait_send()
    for j in range(CHUNKS):
        source_cross_a(j).wait_send()
        for side in (0, 1):
            for p in range(PIECES):
                halo_copy(j, side, p).wait_send()
            source_halo(j, side).wait_send()
        cross_y(j).wait_send()

        @pl.when(jnp.logical_not(last_chip))
        def _():
            for p in range(PIECES):
                main_copy(j, p).wait_send()

    for d in range(1, ny):
        y_copy(d).wait_send()
    for d in range(1, nz):
        z_copy(d).wait_send()

    row = lax.broadcasted_iota(jnp.int32, (K, 128), 0)
    scaled = jnp.concatenate([acc, pltpu.roll(acc, 64, 1)], axis=0) * (1.0 / count)
    w = jnp.where(lane < K, scaled, jnp.where(lane == row + 64, 1.0, 0.0))
    for start in range(0, K, BLOCK):
        columns = [jnp.broadcast_to(w[:, start + b:start + b + 1], (K, 128)) for b in range(BLOCK)]
        for b in range(BLOCK):
            j = start + b
            inverse = lax.rsqrt(columns[b][j:j + 1, :])
            unit = w[j:j + 1, :] * inverse
            column = jnp.where(row > j, columns[b] * inverse, 0.0)
            for later in range(b + 1, BLOCK):
                columns[later] = columns[later] - column * (columns[later][j:j + 1, :] * inverse)
            w = jnp.where(row == j, unit, w - column * unit)
    w_ref[...] = w


def basis_kernel(lz, yt, w_ref, o_ref, u_ref):
    rows = lz * KC
    w = w_ref[...]
    lane = lax.broadcasted_iota(jnp.int32, (K, 128), 1)
    row = lax.broadcasted_iota(jnp.int32, (K, 128), 0)
    u_ref[...] = jnp.where(lane >= row, w, 0.0)[:, :K]
    tile_row = lax.broadcasted_iota(jnp.int32, (K, lz * K), 0)
    tile_lane = lax.broadcasted_iota(jnp.int32, (K, lz * K), 1)
    copies = (tile_row == lax.rem(tile_lane, K)).astype(F32).astype(BF)
    high = w.astype(BF)
    low = (w - high.astype(F32)).astype(BF)
    block_row = lax.broadcasted_iota(jnp.int32, (rows, lz * K), 0)
    block_lane = lax.broadcasted_iota(jnp.int32, (rows, lz * K), 1)
    same = block_row // KC == block_lane // K
    out = None
    for part in (high, low):
        tiled = lax.dot_general(part, copies, (((0,), (0,)), ((), ())), preferred_element_type=F32)
        blocks = []
        for c in range(2 * CHUNKS):
            one = tiled[64 + c * KC:64 + (c + 1) * KC]
            blocks.append(jnp.where(same, jnp.concatenate([one] * lz, axis=0), 0.0))
        block = jnp.concatenate(blocks, axis=0).astype(BF)
        term = jnp.dot(yt[...], block, preferred_element_type=F32)
        out = term if out is None else out + term
    o_ref[...] = out.astype(BF)


def local(sizes, count, inverse_blocks, coupling, sources):
    ng, ny, nz = sizes
    fn = inverse_blocks.shape[1]
    lz = sources.shape[2] // K
    rows = lz * KC
    half = STATIONS * KC
    hbm = pl.BlockSpec(memory_space=pltpu.HBM)
    vmem = pl.BlockSpec(memory_space=pltpu.VMEM)
    dma = pltpu.SemaphoreType.DMA
    yt, factors = pl.pallas_call(
        functools.partial(march_kernel, sizes, lz, fn, count),
        name="march",
        out_shape=(pltpu.VMEM((fn, lz * K), BF), pltpu.VMEM((K, 128), F32)),
        in_specs=[hbm, hbm, hbm],
        out_specs=(vmem, vmem),
        scratch_shapes=[
            pltpu.VMEM((STATIONS, fn, fn), BF),
            pltpu.VMEM((2, STATIONS, fn, fn), BF),
            pltpu.VMEM((STATIONS, fn), F32),
            pltpu.VMEM((2, 2 * STATIONS, fn), F32),
            pltpu.VMEM((fn, lz * K), BF),
            pltpu.VMEM((CHUNKS, rows, fn), BF),
            pltpu.VMEM((CHUNKS, rows, fn), BF),
            pltpu.VMEM((CHUNKS, 2 * half + rows, fn), BF),
            pltpu.VMEM((CHUNKS, 3 * rows, fn), BF),
            pltpu.VMEM((CHUNKS, rows, fn), BF),
            pltpu.VMEM((3 * rows, fn), BF),
            pltpu.VMEM((3 * rows, fn), BF),
            pltpu.VMEM((2, CHUNKS, rows, fn), BF),
            pltpu.VMEM((2, CHUNKS, rows, fn), BF),
            pltpu.VMEM((ny, K // 2, 128), F32),
            pltpu.VMEM((nz, K // 2, 128), F32),
            dma((STATIONS + 2,)),
            dma((STATIONS,)), dma((STATIONS,)),
            dma((1,)), dma((1,)),
            dma((CHUNKS,)), dma((CHUNKS,)),
            dma((CHUNKS, 2)), dma((CHUNKS, 2)),
            dma((CHUNKS, PIECES)), dma((CHUNKS, PIECES)),
            dma((CHUNKS, 2, PIECES)), dma((CHUNKS, 2, PIECES)),
            dma((CHUNKS,)), dma((CHUNKS,)),
            dma((ny - 1,)), dma((ny - 1,)),
            dma((nz - 1,)), dma((nz - 1,)),
        ],
        compiler_params=pltpu.CompilerParams(collective_id=0, has_side_effects=True, vmem_limit_bytes=60 << 20),
    )(inverse_blocks, coupling, sources[0])
    basis, upper = pl.pallas_call(
        functools.partial(basis_kernel, lz),
        name="basis",
        out_shape=(jax.ShapeDtypeStruct((fn, lz * K), BF), jax.ShapeDtypeStruct((K, K), F32)),
        in_specs=[vmem, vmem],
        out_specs=(vmem, vmem),
        compiler_params=pltpu.CompilerParams(vmem_limit_bytes=32 << 20),
    )(yt, factors)
    return basis[None], upper[None]


def solution(mesh):
    placed = (P("section", None, None), P("section", None), P("section", None, "span"))
    sizes = grid_sizes(mesh)

    def whole(inverse_blocks, coupling, sources):
        count = float(sources.shape[1] * sources.shape[2] // K)
        return jax.shard_map(
            functools.partial(local, sizes, count),
            mesh=mesh,
            in_specs=placed,
            out_specs=(P("section", None, "span"), P("section", None, None)),
            check_vma=False,
        )(inverse_blocks, coupling, sources)

    return whole
```

```python
import functools

import jax
import jax.numpy as jnp
from jax import lax
from jax.experimental import pallas as pl
from jax.experimental.pallas import tpu as pltpu
from jax.sharding import PartitionSpec as P

MESH = pl.DeviceIdType.MESH
K = 48
STATIONS = 4
KC = 8
CHUNKS = 3
PIECES = 3
BLOCK = 8
BF = jnp.bfloat16
F32 = jnp.float32


def grid_sizes(mesh):
    span = mesh.shape["span"]
    rows = 4 if span == 32 else 2
    return mesh.shape["section"], rows, span // rows


def march_kernel(sizes, lz, fn, count, a_hbm, c_hbm, s_hbm, yt, w_ref,
                 av, aw, at, cv, cc, sv, tmp, sa, sb, ext, inc, wa, wb, ym, yf, gy, gz,
                 lsem, wsend, wrecv, csend, crecv, ssend, srecv, bsend, brecv,
                 msend, mrecv, hsend, hrecv, xsend, xrecv, ysend, yrecv, zsend, zrecv):
    ng, ny, nz = sizes
    ns = ny * nz
    rows = lz * KC
    half = STATIONS * KC
    g = lax.axis_index("section")
    s = lax.axis_index("span")
    core = lax.rem(g, 2)
    my, mz = s // nz, lax.rem(s, nz)
    left = (g, lax.rem(s + ns - 1, ns))
    right = (g, lax.rem(s + 1, ns))
    other = (g + 1 - 2 * core, s)
    below = (lax.rem(g + ng - 2, ng), s)
    above = (lax.rem(g + 2, ng), s)
    first_chip = g >= ng - 2
    last_chip = g < 2
    is_one = core == 1
    is_zero = core == 0

    source_copy = pltpu.make_async_copy(s_hbm, sv, lsem.at[STATIONS])
    source_copy.start()
    rate_copy = pltpu.make_async_copy(c_hbm, cv, lsem.at[STATIONS + 1])
    rate_copy.start()
    weight_copies = [pltpu.make_async_copy(a_hbm.at[i], av.at[i], lsem.at[i]) for i in range(STATIONS)]
    for i in reversed(range(STATIONS)):
        weight_copies[i].start()

    barrier = pltpu.get_barrier_semaphore()

    def greet(device):
        pl.semaphore_signal(barrier, inc=1, device_id=device, device_id_type=MESH)

    y_peer = lambda d: (g, lax.rem(my + d, ny) * nz + mz)
    z_peer = lambda d: (g, my * nz + lax.rem(mz + d, nz))
    for device in [left, right, other, below, above]:
        greet(device)
    for d in range(1, ny):
        greet(y_peer(d))
    for d in range(1, nz):
        greet(z_peer(d))

    def remote(src, dst, send, recv, device):
        return pltpu.make_async_remote_copy(
            src_ref=src, dst_ref=dst, send_sem=send, recv_sem=recv, device_id=device, device_id_type=MESH)

    weight_cross = lambda i: remote(a_hbm.at[i], aw.at[i], wsend.at[i], wrecv.at[i], other)
    rate_cross = lambda p: remote(cc.at[p], cc.at[p], csend.at[0], crecv.at[0], other)
    middle = pl.ds(half, rows)
    source_cross_a = lambda j: remote(tmp.at[j], sa.at[j], ssend.at[j], srecv.at[j], other)
    source_cross_b = lambda j: remote(tmp.at[j], sb.at[j, middle], ssend.at[j], srecv.at[j], other)
    width = fn // PIECES
    lanes = lambda p: pl.ds(p * width, width)
    everything = pl.ds(0, rows)

    def main_copy(j, p):
        return remote(ym.at[0, j, everything, lanes(p)], inc.at[j, everything, lanes(p)],
                      msend.at[j, p], mrecv.at[j, p], below)

    cross_y = lambda j: remote(ym.at[1 - core, j], yf.at[core, j], xsend.at[j], xrecv.at[j], other)

    def halo_copy(j, side, p):
        target, device = ((2 * rows, left), (0, right))[side]
        return remote(ext.at[j, pl.ds(rows, rows), lanes(p)], ext.at[j, pl.ds(target, rows), lanes(p)],
                      hsend.at[j, side, p], hrecv.at[j, side, p], device)

    def source_halo(j, side):
        start, target, device = ((half, half + rows, left), (rows, 0, right))[side]
        return remote(sb.at[j, pl.ds(start, half)], sb.at[j, pl.ds(target, half)],
                      bsend.at[j, side], brecv.at[j, side], device)

    source_copy.wait()
    total = 2 * CHUNKS * rows
    pick_row = lax.broadcasted_iota(jnp.int32, (CHUNKS * rows, lz * K), 0)
    pick_lane = lax.broadcasted_iota(jnp.int32, (CHUNKS * rows, lz * K), 1)
    in_chunk = lax.rem(pick_row, rows)
    source_lane = (in_chunk // KC) * K + (pick_row // rows) * KC + lax.rem(in_chunk, KC)

    def columns(h):
        pick = (pick_lane == source_lane + h * (K // 2)).astype(F32).astype(BF)
        moved = lax.dot_general(pick, sv[...], (((1,), (1,)), ((), ())), preferred_element_type=F32)
        return moved.astype(BF).reshape(CHUNKS, rows, fn)

    tmp[...] = columns(1 - core)
    pl.semaphore_wait(barrier, ny + nz + 3)

    for j in range(CHUNKS):
        @pl.when(is_one)
        def _():
            source_cross_a(j).start()

        @pl.when(is_zero)
        def _():
            source_cross_b(j).start()

        weight_cross(STATIONS - 1 - j).start()
    for i in reversed(range(STATIONS - CHUNKS)):
        weight_cross(i).start()
    mine = columns(core)

    @pl.when(is_one)
    def _():
        sa[...] = mine

    @pl.when(is_zero)
    def _():
        sb[:, middle, :] = mine

    def begin(j):
        @pl.when(first_chip)
        def _():
            @pl.when(is_zero)
            def _():
                source_cross_a(j).wait_recv()

            ext[j, pl.ds(rows, rows), :] = sa[j]
            for p in range(PIECES):
                halo_copy(j, 0, p).start()
                halo_copy(j, 1, p).start()

    def share_sources(j):
        @pl.when(is_one)
        def _():
            source_cross_b(j).wait_recv()

        @pl.when(jnp.logical_and(is_zero, jnp.logical_not(first_chip)))
        def _():
            source_cross_a(j).wait_recv()

        source_halo(j, 0).start()
        source_halo(j, 1).start()

    begin(0)
    share_sources(0)
    rate_copy.wait()
    cc[core] = jnp.concatenate([cv[...], jnp.zeros_like(cv)], axis=0)
    rate_cross(core).start()
    for i in reversed(range(STATIONS)):
        weight_copies[i].wait()
        at[core, i] = av[i].T
        if i == STATIONS // 2:
            begin(1)
            share_sources(1)
    begin(2)
    share_sources(2)

    rate_cross(1 - core).wait_recv()

    def receive_weights(i):
        weight_cross(i).wait_recv()
        at[1 - core, i] = aw[i].T

    @pl.when(jnp.logical_not(first_chip))
    def _():
        for i in reversed(range(STATIONS)):
            receive_weights(i)

    def prepare(j):
        @pl.when(jnp.logical_not(first_chip))
        def _():
            for p in range(PIECES):
                main_copy(j, p).wait_recv()
                at_piece = (j, everything, lanes(p))
                ext[j, pl.ds(rows, rows), lanes(p)] = (inc[at_piece].astype(F32) + sa[at_piece].astype(F32)).astype(BF)
                halo_copy(j, 0, p).start()
                halo_copy(j, 1, p).start()

    def arrive(j, p, i):
        @pl.when(jnp.logical_and(jnp.logical_and(j == 0, first_chip), core != p))
        def _():
            receive_weights(i)

    def spread_out(value, rates):
        w = value.astype(F32)
        center = w[KC:-KC]
        spread = w[2 * KC:] + w[:-2 * KC] - 2.0 * center
        return (center + rates * spread).astype(BF)

    def diffuse(j, p, i, value):
        arrive(j, p, i)
        return spread_out(value, cc[p, i:i + 1, :])

    def station(j, p, i, value):
        return jnp.dot(diffuse(j, p, i, value), at[p, i], preferred_element_type=F32).astype(BF)

    def compute(j):
        n = 3 * rows
        step = 2 * KC
        product = None
        for p in range(PIECES):
            halo_copy(j, 0, p).wait_recv()
            halo_copy(j, 1, p).wait_recv()
            if p == 0:
                arrive(j, 1, 3)
            update = spread_out(ext[j, :, lanes(p)], cc[1, 3:4, lanes(p)])
            term = jnp.dot(update, at[1, 3, lanes(p), :], preferred_element_type=F32)
            product = term if product is None else product + term
        wa[pl.ds(0, n - step), :] = product.astype(BF)
        wb[pl.ds(0, n - 2 * step), :] = station(j, 1, 2, wa[pl.ds(0, n - step), :])
        wa[pl.ds(0, n - 3 * step), :] = station(j, 1, 1, wb[pl.ds(0, n - 2 * step), :])
        n = 2 * rows
        upper_out = station(j, 1, 0, wa[pl.ds(0, n + step), :])
        wb[pl.ds(0, n), :] = upper_out
        ym[1, j] = wb[middle, :]

        @pl.when(is_one)
        def _():
            yf[1, j] = ym[1, j]

        @pl.when(is_zero)
        def _():
            cross_y(j).start()

        source_halo(j, 0).wait_recv()
        source_halo(j, 1).wait_recv()
        value = (upper_out.astype(F32) + sb[j].astype(F32)).astype(BF)
        wa[pl.ds(0, n - step), :] = station(j, 0, 3, value)
        wb[pl.ds(0, n - 2 * step), :] = station(j, 0, 2, wa[pl.ds(0, n - step), :])

        @pl.when(j < CHUNKS - 2)
        def _():
            prepare(j + 2)

        wa[pl.ds(0, n - 3 * step), :] = station(j, 0, 1, wb[pl.ds(0, n - 2 * step), :])
        update = diffuse(j, 0, 0, wa[pl.ds(0, n - 3 * step), :])
        for p in range(PIECES):
            ym[0, j, everything, lanes(p)] = jnp.dot(
                update, at[0, 0, :, lanes(p)], preferred_element_type=F32).astype(BF)

            @pl.when(jnp.logical_not(last_chip))
            def _():
                main_copy(j, p).start()

        @pl.when(is_zero)
        def _():
            yf[0, j] = ym[0, j]

        @pl.when(is_one)
        def _():
            cross_y(j).start()

    prepare(0)
    prepare(1)

    def chunk_step(j, carry):
        compute(j)
        return carry

    lax.fori_loop(0, CHUNKS, chunk_step, 0)
    for j in range(CHUNKS):
        cross_y(j).wait_recv()

    flat = yf[...].reshape(total, fn)
    gram = lax.dot_general(flat, flat, (((1,), (1,)), ((), ())), preferred_element_type=F32)
    z_of_row = lax.rem(lax.broadcasted_iota(jnp.int32, (total, total), 0), rows) // KC
    z_of_lane = lax.rem(lax.broadcasted_iota(jnp.int32, (total, total), 1), rows) // KC
    gram = jnp.where(z_of_row == z_of_lane, gram, 0.0)
    gram = gram.reshape(2 * CHUNKS, lz, KC, total).sum(1).reshape(K, total)
    lane = lax.broadcasted_iota(jnp.int32, (K, 128), 1)
    packed = jnp.zeros((K, 128), F32)
    for c in range(2 * CHUNKS):
        pair = gram[:, (c // 2) * 128:(c // 2 + 1) * 128]
        tile = jnp.where(lane // rows == c % 2, pair, 0.0)
        for shift in (64, 32, 16, 8):
            tile = tile + pltpu.roll(tile, shift, 1)
        packed = jnp.where(lane // KC == c, tile, packed)
    first, second, third = packed[:16], packed[16:32], packed[32:]
    top = lax.broadcasted_iota(jnp.int32, (16, 128), 1)
    sides = jnp.where(top < 64, pltpu.roll(third, 16, 1), pltpu.roll(second, 48, 1))
    gy[my] = jnp.where(top < K, first, jnp.where(top < 96, sides, 0.0))

    y_copy = lambda d: remote(gy.at[my], gy.at[my], ysend.at[d - 1], yrecv.at[d - 1], y_peer(d))
    z_copy = lambda d: remote(gz.at[mz], gz.at[mz], zsend.at[d - 1], zrecv.at[d - 1], z_peer(d))

    for d in range(1, ny):
        y_copy(d).start()
    yt[...] = flat.T
    for d in range(1, ny):
        y_copy(d).wait_recv()
    acc = gy[0]
    for i in range(1, ny):
        acc = acc + gy[i]
    gz[mz] = acc
    for d in range(1, nz):
        z_copy(d).start()
    for d in range(1, nz):
        z_copy(d).wait_recv()
    acc = gz[0]
    for i in range(1, nz):
        acc = acc + gz[i]

    rate_cross(core).wait_send()
    for i in range(STATIONS):
        weight_cross(i).wait_send()
    for j in range(CHUNKS):
        source_cross_a(j).wait_send()
        for side in (0, 1):
            for p in range(PIECES):
                halo_copy(j, side, p).wait_send()
            source_halo(j, side).wait_send()
        cross_y(j).wait_send()

        @pl.when(jnp.logical_not(last_chip))
        def _():
            for p in range(PIECES):
                main_copy(j, p).wait_send()

    for d in range(1, ny):
        y_copy(d).wait_send()
    for d in range(1, nz):
        z_copy(d).wait_send()

    row = lax.broadcasted_iota(jnp.int32, (K, 128), 0)
    scaled = jnp.concatenate([acc, pltpu.roll(acc, 80, 1), pltpu.roll(acc, 112, 1)], axis=0) * (1.0 / count)
    upper = jnp.where(jnp.logical_and(lane < K, lane >= row), scaled, 0.0)
    lower = jnp.concatenate([upper, jnp.zeros((128 - K, 128), F32)], axis=0).T[:K]
    w = jnp.where(lane > row, upper, lower) + jnp.where(lane == row + 64, 1.0, 0.0)
    for start in range(0, K, BLOCK):
        columns = [jnp.broadcast_to(w[:, start + b:start + b + 1], (K, 128)) for b in range(BLOCK)]
        for b in range(BLOCK):
            j = start + b
            inverse = lax.rsqrt(columns[b][j:j + 1, :])
            unit = w[j:j + 1, :] * inverse
            column = jnp.where(row > j, columns[b] * inverse, 0.0)
            for later in range(b + 1, BLOCK):
                columns[later] = columns[later] - column * (columns[later][j:j + 1, :] * inverse)
            w = jnp.where(row == j, unit, w - column * unit)
    w_ref[...] = w


def basis_kernel(lz, yt, w_ref, o_ref, u_ref):
    rows = lz * KC
    w = w_ref[...]
    lane = lax.broadcasted_iota(jnp.int32, (K, 128), 1)
    row = lax.broadcasted_iota(jnp.int32, (K, 128), 0)
    u_ref[...] = jnp.where(lane >= row, w, 0.0)[:, :K]
    tile_row = lax.broadcasted_iota(jnp.int32, (K, lz * K), 0)
    tile_lane = lax.broadcasted_iota(jnp.int32, (K, lz * K), 1)
    copies = (tile_row == lax.rem(tile_lane, K)).astype(F32).astype(BF)
    high = w.astype(BF)
    low = (w - high.astype(F32)).astype(BF)
    block_row = lax.broadcasted_iota(jnp.int32, (rows, lz * K), 0)
    block_lane = lax.broadcasted_iota(jnp.int32, (rows, lz * K), 1)
    same = block_row // KC == block_lane // K
    out = None
    for part in (high, low):
        tiled = lax.dot_general(part, copies, (((0,), (0,)), ((), ())), preferred_element_type=F32)
        blocks = []
        for c in range(2 * CHUNKS):
            one = tiled[64 + c * KC:64 + (c + 1) * KC]
            blocks.append(jnp.where(same, jnp.concatenate([one] * lz, axis=0), 0.0))
        block = jnp.concatenate(blocks, axis=0).astype(BF)
        term = jnp.dot(yt[...], block, preferred_element_type=F32)
        out = term if out is None else out + term
    o_ref[...] = out.astype(BF)


def local(sizes, count, inverse_blocks, coupling, sources):
    ng, ny, nz = sizes
    fn = inverse_blocks.shape[1]
    lz = sources.shape[2] // K
    rows = lz * KC
    half = STATIONS * KC
    hbm = pl.BlockSpec(memory_space=pltpu.HBM)
    vmem = pl.BlockSpec(memory_space=pltpu.VMEM)
    dma = pltpu.SemaphoreType.DMA
    yt, factors = pl.pallas_call(
        functools.partial(march_kernel, sizes, lz, fn, count),
        name="march",
        out_shape=(pltpu.VMEM((fn, lz * K), BF), pltpu.VMEM((K, 128), F32)),
        in_specs=[hbm, hbm, hbm],
        out_specs=(vmem, vmem),
        scratch_shapes=[
            pltpu.VMEM((STATIONS, fn, fn), BF),
            pltpu.VMEM((STATIONS, fn, fn), BF),
            pltpu.VMEM((2, STATIONS, fn, fn), BF),
            pltpu.VMEM((STATIONS, fn), F32),
            pltpu.VMEM((2, 2 * STATIONS, fn), F32),
            pltpu.VMEM((fn, lz * K), BF),
            pltpu.VMEM((CHUNKS, rows, fn), BF),
            pltpu.VMEM((CHUNKS, rows, fn), BF),
            pltpu.VMEM((CHUNKS, 2 * half + rows, fn), BF),
            pltpu.VMEM((CHUNKS, 3 * rows, fn), BF),
            pltpu.VMEM((CHUNKS, rows, fn), BF),
            pltpu.VMEM((3 * rows, fn), BF),
            pltpu.VMEM((3 * rows, fn), BF),
            pltpu.VMEM((2, CHUNKS, rows, fn), BF),
            pltpu.VMEM((2, CHUNKS, rows, fn), BF),
            pltpu.VMEM((ny, K // 3, 128), F32),
            pltpu.VMEM((nz, K // 3, 128), F32),
            dma((STATIONS + 2,)),
            dma((STATIONS,)), dma((STATIONS,)),
            dma((1,)), dma((1,)),
            dma((CHUNKS,)), dma((CHUNKS,)),
            dma((CHUNKS, 2)), dma((CHUNKS, 2)),
            dma((CHUNKS, PIECES)), dma((CHUNKS, PIECES)),
            dma((CHUNKS, 2, PIECES)), dma((CHUNKS, 2, PIECES)),
            dma((CHUNKS,)), dma((CHUNKS,)),
            dma((ny - 1,)), dma((ny - 1,)),
            dma((nz - 1,)), dma((nz - 1,)),
        ],
        compiler_params=pltpu.CompilerParams(collective_id=0, has_side_effects=True, vmem_limit_bytes=60 << 20),
    )(inverse_blocks, coupling, sources[0])
    basis, upper = pl.pallas_call(
        functools.partial(basis_kernel, lz),
        name="basis",
        out_shape=(jax.ShapeDtypeStruct((fn, lz * K), BF), jax.ShapeDtypeStruct((K, K), F32)),
        in_specs=[vmem, vmem],
        out_specs=(vmem, vmem),
        compiler_params=pltpu.CompilerParams(vmem_limit_bytes=32 << 20),
    )(yt, factors)
    return basis[None], upper[None]


def solution(mesh):
    placed = (P("section", None, None), P("section", None), P("section", None, "span"))
    sizes = grid_sizes(mesh)

    def whole(inverse_blocks, coupling, sources):
        count = float(sources.shape[1] * sources.shape[2] // K)
        return jax.shard_map(
            functools.partial(local, sizes, count),
            mesh=mesh,
            in_specs=placed,
            out_specs=(P("section", None, "span"), P("section", None, None)),
            check_vma=False,
        )(inverse_blocks, coupling, sources)

    return whole
```

```python
import functools

import jax
import jax.numpy as jnp
from jax import lax
from jax.experimental import pallas as pl
from jax.experimental.pallas import tpu as pltpu
from jax.sharding import PartitionSpec as P

MESH = pl.DeviceIdType.MESH
K = 48
STATIONS = 4
KC = 8
CHUNKS = 3
PIECES = 3
BLOCK = 8
BF = jnp.bfloat16
F32 = jnp.float32


def grid_sizes(mesh):
    span = mesh.shape["span"]
    rows = 4 if span == 32 else 2
    return mesh.shape["section"], rows, span // rows


def march_kernel(sizes, lz, fn, count, a_hbm, c_hbm, s_hbm, yt, w_ref,
                 av, aw, at, cv, cc, sv, tmp, sa, sb, ext, inc, wa, wb, ym, yf, gy, gz,
                 lsem, wsend, wrecv, csend, crecv, ssend, srecv, bsend, brecv,
                 msend, mrecv, hsend, hrecv, xsend, xrecv, ysend, yrecv, zsend, zrecv):
    ng, ny, nz = sizes
    ns = ny * nz
    rows = lz * KC
    half = STATIONS * KC
    g = lax.axis_index("section")
    s = lax.axis_index("span")
    core = lax.rem(g, 2)
    my, mz = s // nz, lax.rem(s, nz)
    left = (g, lax.rem(s + ns - 1, ns))
    right = (g, lax.rem(s + 1, ns))
    other = (g + 1 - 2 * core, s)
    below = (lax.rem(g + ng - 2, ng), s)
    above = (lax.rem(g + 2, ng), s)
    first_chip = g >= ng - 2
    last_chip = g < 2
    is_one = core == 1
    is_zero = core == 0

    source_copy = pltpu.make_async_copy(s_hbm, sv, lsem.at[STATIONS])
    source_copy.start()
    rate_copy = pltpu.make_async_copy(c_hbm, cv, lsem.at[STATIONS + 1])
    rate_copy.start()
    weight_copies = [pltpu.make_async_copy(a_hbm.at[i], av.at[i], lsem.at[i]) for i in range(STATIONS)]
    for i in reversed(range(STATIONS)):
        weight_copies[i].start()

    barrier = pltpu.get_barrier_semaphore()

    def greet(device):
        pl.semaphore_signal(barrier, inc=1, device_id=device, device_id_type=MESH)

    y_peer = lambda d: (g, lax.rem(my + d, ny) * nz + mz)
    z_peer = lambda d: (g, my * nz + lax.rem(mz + d, nz))
    for device in [left, right, other, below, above]:
        greet(device)
    for d in range(1, ny):
        greet(y_peer(d))
    for d in range(1, nz):
        greet(z_peer(d))

    def remote(src, dst, send, recv, device):
        return pltpu.make_async_remote_copy(
            src_ref=src, dst_ref=dst, send_sem=send, recv_sem=recv, device_id=device, device_id_type=MESH)

    early = STATIONS // 2

    def weight_cross(p, i):
        if i >= early:
            return remote(a_hbm.at[i], aw.at[i - early], wsend.at[i], wrecv.at[i], other)
        return remote(at.at[p, i], at.at[p, i], wsend.at[i], wrecv.at[i], other)

    rate_cross = lambda p: remote(cc.at[p], cc.at[p], csend.at[0], crecv.at[0], other)
    middle = pl.ds(half, rows)
    source_cross_a = lambda j: remote(tmp.at[j], sa.at[j], ssend.at[j], srecv.at[j], other)
    source_cross_b = lambda j: remote(tmp.at[j], sb.at[j, middle], ssend.at[j], srecv.at[j], other)
    width = fn // PIECES
    lanes = lambda p: pl.ds(p * width, width)
    everything = pl.ds(0, rows)

    def main_copy(j, p):
        return remote(ym.at[0, j, everything, lanes(p)], inc.at[j, everything, lanes(p)],
                      msend.at[j, p], mrecv.at[j, p], below)

    cross_y = lambda j: remote(ym.at[1 - core, j], yf.at[core, j], xsend.at[j], xrecv.at[j], other)

    def halo_copy(j, side, p):
        target, device = ((2 * rows, left), (0, right))[side]
        return remote(ext.at[j, pl.ds(rows, rows), lanes(p)], ext.at[j, pl.ds(target, rows), lanes(p)],
                      hsend.at[j, side, p], hrecv.at[j, side, p], device)

    def source_halo(j, side):
        start, target, device = ((half, half + rows, left), (rows, 0, right))[side]
        return remote(sb.at[j, pl.ds(start, half)], sb.at[j, pl.ds(target, half)],
                      bsend.at[j, side], brecv.at[j, side], device)

    source_copy.wait()
    total = 2 * CHUNKS * rows
    pick_row = lax.broadcasted_iota(jnp.int32, (CHUNKS * rows, lz * K), 0)
    pick_lane = lax.broadcasted_iota(jnp.int32, (CHUNKS * rows, lz * K), 1)
    in_chunk = lax.rem(pick_row, rows)
    source_lane = (in_chunk // KC) * K + (pick_row // rows) * KC + lax.rem(in_chunk, KC)

    def columns(h):
        pick = (pick_lane == source_lane + h * (K // 2)).astype(F32).astype(BF)
        moved = lax.dot_general(pick, sv[...], (((1,), (1,)), ((), ())), preferred_element_type=F32)
        return moved.astype(BF).reshape(CHUNKS, rows, fn)

    tmp[...] = columns(1 - core)
    pl.semaphore_wait(barrier, ny + nz + 3)

    for j in range(CHUNKS):
        @pl.when(is_one)
        def _():
            source_cross_a(j).start()

        @pl.when(is_zero)
        def _():
            source_cross_b(j).start()

        if j < STATIONS - early:
            weight_cross(core, STATIONS - 1 - j).start()
    mine = columns(core)

    @pl.when(is_one)
    def _():
        sa[...] = mine

    @pl.when(is_zero)
    def _():
        sb[:, middle, :] = mine

    def begin(j):
        @pl.when(first_chip)
        def _():
            @pl.when(is_zero)
            def _():
                source_cross_a(j).wait_recv()

            ext[j, pl.ds(rows, rows), :] = sa[j]
            for p in range(PIECES):
                halo_copy(j, 0, p).start()
                halo_copy(j, 1, p).start()

    def share_sources(j):
        @pl.when(is_one)
        def _():
            source_cross_b(j).wait_recv()

        @pl.when(jnp.logical_and(is_zero, jnp.logical_not(first_chip)))
        def _():
            source_cross_a(j).wait_recv()

        source_halo(j, 0).start()
        source_halo(j, 1).start()

    begin(0)
    share_sources(0)
    rate_copy.wait()
    cc[core] = jnp.concatenate([cv[...], jnp.zeros_like(cv)], axis=0)
    rate_cross(core).start()
    for i in reversed(range(STATIONS)):
        weight_copies[i].wait()
        at[core, i] = av[i].T
        if i < early:
            weight_cross(core, i).start()
        if i == early:
            begin(1)
            share_sources(1)
    begin(2)
    share_sources(2)

    rate_cross(1 - core).wait_recv()

    for i in reversed(range(early, STATIONS)):
        weight_cross(1 - core, i).wait_recv()
        at[1 - core, i] = aw[i - early].T

    @pl.when(jnp.logical_not(first_chip))
    def _():
        for i in reversed(range(early)):
            weight_cross(1 - core, i).wait_recv()

    def prepare(j):
        @pl.when(jnp.logical_not(first_chip))
        def _():
            for p in range(PIECES):
                main_copy(j, p).wait_recv()
                at_piece = (j, everything, lanes(p))
                ext[j, pl.ds(rows, rows), lanes(p)] = (inc[at_piece].astype(F32) + sa[at_piece].astype(F32)).astype(BF)
                halo_copy(j, 0, p).start()
                halo_copy(j, 1, p).start()

    def arrive(first, p, i):
        if first and i < early:
            @pl.when(jnp.logical_and(first_chip, core != p))
            def _():
                weight_cross(p, i).wait_recv()

    def spread_out(value, rates):
        w = value.astype(F32)
        center = w[KC:-KC]
        spread = w[2 * KC:] + w[:-2 * KC] - 2.0 * center
        return (center + rates * spread).astype(BF)

    def diffuse(first, p, i, value):
        arrive(first, p, i)
        return spread_out(value, cc[p, i:i + 1, :])

    def station(first, p, i, value):
        return jnp.dot(diffuse(first, p, i, value), at[p, i], preferred_element_type=F32).astype(BF)

    def compute(j, first):
        n = 3 * rows
        step = 2 * KC
        product = None
        for p in range(PIECES):
            halo_copy(j, 0, p).wait_recv()
            halo_copy(j, 1, p).wait_recv()
            update = spread_out(ext[j, :, lanes(p)], cc[1, 3:4, lanes(p)])
            term = jnp.dot(update, at[1, 3, lanes(p), :], preferred_element_type=F32)
            product = term if product is None else product + term
        wa[pl.ds(0, n - step), :] = product.astype(BF)
        wb[pl.ds(0, n - 2 * step), :] = station(first, 1, 2, wa[pl.ds(0, n - step), :])
        wa[pl.ds(0, n - 3 * step), :] = station(first, 1, 1, wb[pl.ds(0, n - 2 * step), :])
        n = 2 * rows
        upper_out = station(first, 1, 0, wa[pl.ds(0, n + step), :])
        wb[pl.ds(0, n), :] = upper_out
        ym[1, j] = wb[middle, :]

        @pl.when(is_zero)
        def _():
            cross_y(j).start()

        source_halo(j, 0).wait_recv()
        source_halo(j, 1).wait_recv()
        value = (upper_out.astype(F32) + sb[j].astype(F32)).astype(BF)
        wa[pl.ds(0, n - step), :] = station(first, 0, 3, value)
        wb[pl.ds(0, n - 2 * step), :] = station(first, 0, 2, wa[pl.ds(0, n - step), :])

        if first:
            prepare(2)
        wa[pl.ds(0, n - 3 * step), :] = station(first, 0, 1, wb[pl.ds(0, n - 2 * step), :])
        update = diffuse(first, 0, 0, wa[pl.ds(0, n - 3 * step), :])
        for p in range(PIECES):
            ym[0, j, everything, lanes(p)] = jnp.dot(
                update, at[0, 0, :, lanes(p)], preferred_element_type=F32).astype(BF)

            @pl.when(jnp.logical_not(last_chip))
            def _():
                main_copy(j, p).start()

        yf[core, j] = ym[core, j]

        @pl.when(is_one)
        def _():
            cross_y(j).start()

    prepare(0)
    prepare(1)

    compute(0, True)

    def chunk_step(j, carry):
        compute(j, False)
        return carry

    lax.fori_loop(1, CHUNKS, chunk_step, 0)
    for j in range(CHUNKS):
        cross_y(j).wait_recv()

    flat = yf[...].reshape(total, fn)
    gram = lax.dot_general(flat, flat, (((1,), (1,)), ((), ())), preferred_element_type=F32)
    z_of_row = lax.rem(lax.broadcasted_iota(jnp.int32, (total, total), 0), rows) // KC
    z_of_lane = lax.rem(lax.broadcasted_iota(jnp.int32, (total, total), 1), rows) // KC
    gram = jnp.where(z_of_row == z_of_lane, gram, 0.0)
    gram = gram.reshape(2 * CHUNKS, lz, KC, total).sum(1).reshape(K, total)
    lane = lax.broadcasted_iota(jnp.int32, (K, 128), 1)
    packed = jnp.zeros((K, 128), F32)
    for c in range(2 * CHUNKS):
        pair = gram[:, (c // 2) * 128:(c // 2 + 1) * 128]
        tile = jnp.where(lane // rows == c % 2, pair, 0.0)
        for shift in (64, 32, 16, 8):
            tile = tile + pltpu.roll(tile, shift, 1)
        packed = jnp.where(lane // KC == c, tile, packed)
    first, second, third = packed[:16], packed[16:32], packed[32:]
    top = lax.broadcasted_iota(jnp.int32, (16, 128), 1)
    sides = jnp.where(top < 64, pltpu.roll(third, 16, 1), pltpu.roll(second, 48, 1))
    gy[my] = jnp.where(top < K, first, jnp.where(top < 96, sides, 0.0))

    y_copy = lambda d: remote(gy.at[my], gy.at[my], ysend.at[d - 1], yrecv.at[d - 1], y_peer(d))
    z_copy = lambda d: remote(gz.at[mz], gz.at[mz], zsend.at[d - 1], zrecv.at[d - 1], z_peer(d))

    for d in range(1, ny):
        y_copy(d).start()
    yt[...] = flat.T
    for d in range(1, ny):
        y_copy(d).wait_recv()
    acc = gy[0]
    for i in range(1, ny):
        acc = acc + gy[i]
    gz[mz] = acc
    for d in range(1, nz):
        z_copy(d).start()
    for d in range(1, nz):
        z_copy(d).wait_recv()
    acc = gz[0]
    for i in range(1, nz):
        acc = acc + gz[i]

    rate_cross(core).wait_send()
    for i in range(STATIONS):
        weight_cross(core, i).wait_send()
    for j in range(CHUNKS):
        source_cross_a(j).wait_send()
        for side in (0, 1):
            for p in range(PIECES):
                halo_copy(j, side, p).wait_send()
            source_halo(j, side).wait_send()
        cross_y(j).wait_send()

        @pl.when(jnp.logical_not(last_chip))
        def _():
            for p in range(PIECES):
                main_copy(j, p).wait_send()

    for d in range(1, ny):
        y_copy(d).wait_send()
    for d in range(1, nz):
        z_copy(d).wait_send()

    row = lax.broadcasted_iota(jnp.int32, (K, 128), 0)
    scaled = jnp.concatenate([acc, pltpu.roll(acc, 80, 1), pltpu.roll(acc, 112, 1)], axis=0) * (1.0 / count)
    upper = jnp.where(jnp.logical_and(lane < K, lane >= row), scaled, 0.0)
    lower = jnp.concatenate([upper, jnp.zeros((128 - K, 128), F32)], axis=0).T[:K]
    w = jnp.where(lane > row, upper, lower) + jnp.where(lane == row + 64, 1.0, 0.0)
    for start in range(0, K, BLOCK):
        columns = [jnp.broadcast_to(w[:, start + b:start + b + 1], (K, 128)) for b in range(BLOCK)]
        for b in range(BLOCK):
            j = start + b
            inverse = lax.rsqrt(columns[b][j:j + 1, :])
            unit = w[j:j + 1, :] * inverse
            column = jnp.where(row > j, columns[b] * inverse, 0.0)
            for later in range(b + 1, BLOCK):
                columns[later] = columns[later] - column * (columns[later][j:j + 1, :] * inverse)
            w = jnp.where(row == j, unit, w - column * unit)
    w_ref[...] = w


def basis_kernel(lz, yt, w_ref, o_ref, u_ref):
    rows = lz * KC
    w = w_ref[...]
    lane = lax.broadcasted_iota(jnp.int32, (K, 128), 1)
    row = lax.broadcasted_iota(jnp.int32, (K, 128), 0)
    u_ref[...] = jnp.where(lane >= row, w, 0.0)[:, :K]
    tile_row = lax.broadcasted_iota(jnp.int32, (K, lz * K), 0)
    tile_lane = lax.broadcasted_iota(jnp.int32, (K, lz * K), 1)
    copies = (tile_row == lax.rem(tile_lane, K)).astype(F32).astype(BF)
    high = w.astype(BF)
    low = (w - high.astype(F32)).astype(BF)
    block_row = lax.broadcasted_iota(jnp.int32, (rows, lz * K), 0)
    block_lane = lax.broadcasted_iota(jnp.int32, (rows, lz * K), 1)
    same = block_row // KC == block_lane // K
    out = None
    for part in (high, low):
        tiled = lax.dot_general(part, copies, (((0,), (0,)), ((), ())), preferred_element_type=F32)
        blocks = []
        for c in range(2 * CHUNKS):
            one = tiled[64 + c * KC:64 + (c + 1) * KC]
            blocks.append(jnp.where(same, jnp.concatenate([one] * lz, axis=0), 0.0))
        block = jnp.concatenate(blocks, axis=0).astype(BF)
        term = jnp.dot(yt[...], block, preferred_element_type=F32)
        out = term if out is None else out + term
    o_ref[...] = out.astype(BF)


def local(sizes, count, inverse_blocks, coupling, sources):
    ng, ny, nz = sizes
    fn = inverse_blocks.shape[1]
    lz = sources.shape[2] // K
    rows = lz * KC
    half = STATIONS * KC
    hbm = pl.BlockSpec(memory_space=pltpu.HBM)
    vmem = pl.BlockSpec(memory_space=pltpu.VMEM)
    dma = pltpu.SemaphoreType.DMA
    yt, factors = pl.pallas_call(
        functools.partial(march_kernel, sizes, lz, fn, count),
        name="march",
        out_shape=(pltpu.VMEM((fn, lz * K), BF), pltpu.VMEM((K, 128), F32)),
        in_specs=[hbm, hbm, hbm],
        out_specs=(vmem, vmem),
        scratch_shapes=[
            pltpu.VMEM((STATIONS, fn, fn), BF),
            pltpu.VMEM((STATIONS - STATIONS // 2, fn, fn), BF),
            pltpu.VMEM((2, STATIONS, fn, fn), BF),
            pltpu.VMEM((STATIONS, fn), F32),
            pltpu.VMEM((2, 2 * STATIONS, fn), F32),
            pltpu.VMEM((fn, lz * K), BF),
            pltpu.VMEM((CHUNKS, rows, fn), BF),
            pltpu.VMEM((CHUNKS, rows, fn), BF),
            pltpu.VMEM((CHUNKS, 2 * half + rows, fn), BF),
            pltpu.VMEM((CHUNKS, 3 * rows, fn), BF),
            pltpu.VMEM((CHUNKS, rows, fn), BF),
            pltpu.VMEM((3 * rows, fn), BF),
            pltpu.VMEM((3 * rows, fn), BF),
            pltpu.VMEM((2, CHUNKS, rows, fn), BF),
            pltpu.VMEM((2, CHUNKS, rows, fn), BF),
            pltpu.VMEM((ny, K // 3, 128), F32),
            pltpu.VMEM((nz, K // 3, 128), F32),
            dma((STATIONS + 2,)),
            dma((STATIONS,)), dma((STATIONS,)),
            dma((1,)), dma((1,)),
            dma((CHUNKS,)), dma((CHUNKS,)),
            dma((CHUNKS, 2)), dma((CHUNKS, 2)),
            dma((CHUNKS, PIECES)), dma((CHUNKS, PIECES)),
            dma((CHUNKS, 2, PIECES)), dma((CHUNKS, 2, PIECES)),
            dma((CHUNKS,)), dma((CHUNKS,)),
            dma((ny - 1,)), dma((ny - 1,)),
            dma((nz - 1,)), dma((nz - 1,)),
        ],
        compiler_params=pltpu.CompilerParams(collective_id=0, has_side_effects=True, vmem_limit_bytes=60 << 20),
    )(inverse_blocks, coupling, sources[0])
    basis, upper = pl.pallas_call(
        functools.partial(basis_kernel, lz),
        name="basis",
        out_shape=(jax.ShapeDtypeStruct((fn, lz * K), BF), jax.ShapeDtypeStruct((K, K), F32)),
        in_specs=[vmem, vmem],
        out_specs=(vmem, vmem),
        compiler_params=pltpu.CompilerParams(vmem_limit_bytes=32 << 20),
    )(yt, factors)
    return basis[None], upper[None]


def solution(mesh):
    placed = (P("section", None, None), P("section", None), P("section", None, "span"))
    sizes = grid_sizes(mesh)

    def whole(inverse_blocks, coupling, sources):
        count = float(sources.shape[1] * sources.shape[2] // K)
        return jax.shard_map(
            functools.partial(local, sizes, count),
            mesh=mesh,
            in_specs=placed,
            out_specs=(P("section", None, "span"), P("section", None, None)),
            check_vma=False,
        )(inverse_blocks, coupling, sources)

    return whole
```

```python
import functools

import jax
import jax.numpy as jnp
from jax import lax
from jax.experimental import pallas as pl
from jax.experimental.pallas import tpu as pltpu
from jax.sharding import PartitionSpec as P

MESH = pl.DeviceIdType.MESH
K = 48
STATIONS = 4
KC = 8
CHUNKS = 3
PIECES = 3
BLOCK = 8
BF = jnp.bfloat16
F32 = jnp.float32


def grid_sizes(mesh):
    span = mesh.shape["span"]
    rows = 4 if span == 32 else 2
    return mesh.shape["section"], rows, span // rows


def march_kernel(sizes, lz, fn, count, a_hbm, c_hbm, s_hbm, yt, w_ref,
                 av, aw, at, cv, cc, sv, tmp, sa, sb, ext, inc, wa, wb, ym, yf, gy, gz,
                 lsem, wsend, wrecv, csend, crecv, ssend, srecv, bsend, brecv,
                 msend, mrecv, hsend, hrecv, xsend, xrecv, ysend, yrecv, zsend, zrecv):
    ng, ny, nz = sizes
    ns = ny * nz
    rows = lz * KC
    half = STATIONS * KC
    g = lax.axis_index("section")
    s = lax.axis_index("span")
    core = lax.rem(g, 2)
    my, mz = s // nz, lax.rem(s, nz)
    left = (g, lax.rem(s + ns - 1, ns))
    right = (g, lax.rem(s + 1, ns))
    other = (g + 1 - 2 * core, s)
    below = (lax.rem(g + ng - 2, ng), s)
    above = (lax.rem(g + 2, ng), s)
    first_chip = g >= ng - 2
    last_chip = g < 2
    is_one = core == 1
    is_zero = core == 0

    source_copy = pltpu.make_async_copy(s_hbm, sv, lsem.at[STATIONS])
    source_copy.start()
    rate_copy = pltpu.make_async_copy(c_hbm, cv, lsem.at[STATIONS + 1])
    rate_copy.start()
    weight_copies = [pltpu.make_async_copy(a_hbm.at[i], av.at[i], lsem.at[i]) for i in range(STATIONS)]
    for i in reversed(range(STATIONS)):
        weight_copies[i].start()

    barrier = pltpu.get_barrier_semaphore()

    def greet(device):
        pl.semaphore_signal(barrier, inc=1, device_id=device, device_id_type=MESH)

    y_peer = lambda d: (g, lax.rem(my + d, ny) * nz + mz)
    z_peer = lambda d: (g, my * nz + lax.rem(mz + d, nz))
    for device in [left, right, other, below, above]:
        greet(device)
    for d in range(1, ny):
        greet(y_peer(d))
    for d in range(1, nz):
        greet(z_peer(d))

    def remote(src, dst, send, recv, device):
        return pltpu.make_async_remote_copy(
            src_ref=src, dst_ref=dst, send_sem=send, recv_sem=recv, device_id=device, device_id_type=MESH)

    early = STATIONS // 2

    def weight_cross(p, i):
        if i >= early:
            return remote(av.at[i], aw.at[i - early], wsend.at[i], wrecv.at[i], other)
        return remote(at.at[p, i], at.at[p, i], wsend.at[i], wrecv.at[i], other)

    rate_cross = lambda p: remote(cc.at[p], cc.at[p], csend.at[0], crecv.at[0], other)
    middle = pl.ds(half, rows)
    source_cross_a = lambda j: remote(tmp.at[j], sa.at[j], ssend.at[j], srecv.at[j], other)
    source_cross_b = lambda j: remote(tmp.at[j], sb.at[j, middle], ssend.at[j], srecv.at[j], other)
    width = fn // PIECES
    lanes = lambda p: pl.ds(p * width, width)
    everything = pl.ds(0, rows)

    def main_copy(j, p):
        return remote(ym.at[0, j, everything, lanes(p)], inc.at[j, everything, lanes(p)],
                      msend.at[j, p], mrecv.at[j, p], below)

    cross_y = lambda j: remote(ym.at[1 - core, j], yf.at[core, j], xsend.at[j], xrecv.at[j], other)

    def halo_copy(j, side, p):
        target, device = ((2 * rows, left), (0, right))[side]
        return remote(ext.at[j, pl.ds(rows, rows), lanes(p)], ext.at[j, pl.ds(target, rows), lanes(p)],
                      hsend.at[j, side, p], hrecv.at[j, side, p], device)

    def source_halo(j, side):
        start, target, device = ((half, half + rows, left), (rows, 0, right))[side]
        return remote(sb.at[j, pl.ds(start, half)], sb.at[j, pl.ds(target, half)],
                      bsend.at[j, side], brecv.at[j, side], device)

    source_copy.wait()
    total = 2 * CHUNKS * rows
    pick_row = lax.broadcasted_iota(jnp.int32, (CHUNKS * rows, lz * K), 0)
    pick_lane = lax.broadcasted_iota(jnp.int32, (CHUNKS * rows, lz * K), 1)
    in_chunk = lax.rem(pick_row, rows)
    source_lane = (in_chunk // KC) * K + (pick_row // rows) * KC + lax.rem(in_chunk, KC)

    def columns(h):
        pick = (pick_lane == source_lane + h * (K // 2)).astype(F32).astype(BF)
        moved = lax.dot_general(pick, sv[...], (((1,), (1,)), ((), ())), preferred_element_type=F32)
        return moved.astype(BF).reshape(CHUNKS, rows, fn)

    tmp[...] = columns(1 - core)
    pl.semaphore_wait(barrier, ny + nz + 3)

    for j in range(CHUNKS):
        @pl.when(is_one)
        def _():
            source_cross_a(j).start()

        @pl.when(is_zero)
        def _():
            source_cross_b(j).start()

        if j < STATIONS - early:
            weight_copies[STATIONS - 1 - j].wait()
            weight_cross(core, STATIONS - 1 - j).start()
    mine = columns(core)

    @pl.when(is_one)
    def _():
        sa[...] = mine

    @pl.when(is_zero)
    def _():
        sb[:, middle, :] = mine

    def begin(j):
        @pl.when(first_chip)
        def _():
            @pl.when(is_zero)
            def _():
                source_cross_a(j).wait_recv()

            ext[j, pl.ds(rows, rows), :] = sa[j]
            for p in range(PIECES):
                halo_copy(j, 0, p).start()
                halo_copy(j, 1, p).start()

    def share_sources(j):
        @pl.when(is_one)
        def _():
            source_cross_b(j).wait_recv()

        @pl.when(jnp.logical_and(is_zero, jnp.logical_not(first_chip)))
        def _():
            source_cross_a(j).wait_recv()

        source_halo(j, 0).start()
        source_halo(j, 1).start()

    begin(0)
    share_sources(0)
    rate_copy.wait()
    cc[core] = jnp.concatenate([cv[...], jnp.zeros_like(cv)], axis=0)
    rate_cross(core).start()
    for i in reversed(range(STATIONS)):
        if i < early:
            weight_copies[i].wait()
        at[core, i] = av[i].T
        if i < early:
            weight_cross(core, i).start()
        if i == early:
            begin(1)
            share_sources(1)
    begin(2)
    share_sources(2)

    rate_cross(1 - core).wait_recv()

    for i in reversed(range(early, STATIONS)):
        weight_cross(1 - core, i).wait_recv()
        at[1 - core, i] = aw[i - early].T

    @pl.when(jnp.logical_not(first_chip))
    def _():
        for i in reversed(range(early)):
            weight_cross(1 - core, i).wait_recv()

    def prepare(j):
        @pl.when(jnp.logical_not(first_chip))
        def _():
            for p in range(PIECES):
                main_copy(j, p).wait_recv()
                at_piece = (j, everything, lanes(p))
                ext[j, pl.ds(rows, rows), lanes(p)] = (inc[at_piece].astype(F32) + sa[at_piece].astype(F32)).astype(BF)
                halo_copy(j, 0, p).start()
                halo_copy(j, 1, p).start()

    def arrive(first, p, i):
        if first and i < early:
            @pl.when(jnp.logical_and(first_chip, core != p))
            def _():
                weight_cross(p, i).wait_recv()

    def spread_out(value, rates):
        w = value.astype(F32)
        center = w[KC:-KC]
        spread = w[2 * KC:] + w[:-2 * KC] - 2.0 * center
        return (center + rates * spread).astype(BF)

    def diffuse(first, p, i, value):
        arrive(first, p, i)
        return spread_out(value, cc[p, i:i + 1, :])

    def station(first, p, i, value):
        return jnp.dot(diffuse(first, p, i, value), at[p, i], preferred_element_type=F32).astype(BF)

    def compute(j, first):
        n = 3 * rows
        step = 2 * KC
        product = None
        for p in range(PIECES):
            halo_copy(j, 0, p).wait_recv()
            halo_copy(j, 1, p).wait_recv()
            update = spread_out(ext[j, :, lanes(p)], cc[1, 3:4, lanes(p)])
            term = jnp.dot(update, at[1, 3, lanes(p), :], preferred_element_type=F32)
            product = term if product is None else product + term
        wa[pl.ds(0, n - step), :] = product.astype(BF)
        wb[pl.ds(0, n - 2 * step), :] = station(first, 1, 2, wa[pl.ds(0, n - step), :])
        wa[pl.ds(0, n - 3 * step), :] = station(first, 1, 1, wb[pl.ds(0, n - 2 * step), :])
        n = 2 * rows
        upper_out = station(first, 1, 0, wa[pl.ds(0, n + step), :])
        wb[pl.ds(0, n), :] = upper_out
        ym[1, j] = wb[middle, :]

        @pl.when(is_zero)
        def _():
            cross_y(j).start()

        source_halo(j, 0).wait_recv()
        source_halo(j, 1).wait_recv()
        value = (upper_out.astype(F32) + sb[j].astype(F32)).astype(BF)
        wa[pl.ds(0, n - step), :] = station(first, 0, 3, value)
        wb[pl.ds(0, n - 2 * step), :] = station(first, 0, 2, wa[pl.ds(0, n - step), :])

        wa[pl.ds(0, n - 3 * step), :] = station(first, 0, 1, wb[pl.ds(0, n - 2 * step), :])
        if first:
            prepare(2)
        update = diffuse(first, 0, 0, wa[pl.ds(0, n - 3 * step), :])
        for p in range(PIECES):
            ym[0, j, everything, lanes(p)] = jnp.dot(
                update, at[0, 0, :, lanes(p)], preferred_element_type=F32).astype(BF)

            @pl.when(jnp.logical_not(last_chip))
            def _():
                main_copy(j, p).start()

        yf[core, j] = ym[core, j]

        @pl.when(is_one)
        def _():
            cross_y(j).start()

    prepare(0)
    prepare(1)

    compute(0, True)

    def chunk_step(j, carry):
        compute(j, False)
        return carry

    lax.fori_loop(1, CHUNKS, chunk_step, 0)
    for j in range(CHUNKS):
        cross_y(j).wait_recv()

    flat = yf[...].reshape(total, fn)
    gram = lax.dot_general(flat, flat, (((1,), (1,)), ((), ())), preferred_element_type=F32)
    group = (lax.broadcasted_iota(jnp.int32, (KC, total), 1) & (rows - 1)) // KC
    parts = []
    for c in range(2 * CHUNKS):
        part = None
        for z in range(lz):
            first = c * rows + z * KC
            one = jnp.where(group == z, gram[first:first + KC], 0.0)
            part = one if part is None else part + one
        parts.append(part)
    gram = jnp.concatenate(parts, axis=0)
    lane = lax.broadcasted_iota(jnp.int32, (K, 128), 1)
    packed = jnp.zeros((K, 128), F32)
    for pair in range(CHUNKS):
        tile = gram[:, pair * 128:(pair + 1) * 128]
        for shift in (32, 16, 8):
            tile = tile + pltpu.roll(tile, shift, 1)
        for c in (2 * pair, 2 * pair + 1):
            end = (c % 2) * rows + rows - KC
            moved = pltpu.roll(tile, (c * KC - end) % 128, 1)
            packed = jnp.where(lane // KC == c, moved, packed)
    first, second, third = packed[:16], packed[16:32], packed[32:]
    top = lax.broadcasted_iota(jnp.int32, (16, 128), 1)
    sides = jnp.where(top < 64, pltpu.roll(third, 16, 1), pltpu.roll(second, 48, 1))
    gy[my] = jnp.where(top < K, first, jnp.where(top < 96, sides, 0.0))

    y_copy = lambda d: remote(gy.at[my], gy.at[my], ysend.at[d - 1], yrecv.at[d - 1], y_peer(d))
    z_copy = lambda d: remote(gz.at[mz], gz.at[mz], zsend.at[d - 1], zrecv.at[d - 1], z_peer(d))

    for d in sorted(range(1, ny), key=lambda d: -min(d, ny - d)):
        y_copy(d).start()
    yt[...] = flat.T
    for d in range(1, ny):
        y_copy(d).wait_recv()
    acc = gy[0]
    for i in range(1, ny):
        acc = acc + gy[i]
    gz[mz] = acc
    for d in sorted(range(1, nz), key=lambda d: -min(d, nz - d)):
        z_copy(d).start()
    for d in range(1, nz):
        z_copy(d).wait_recv()
    acc = gz[0]
    for i in range(1, nz):
        acc = acc + gz[i]

    rate_cross(core).wait_send()
    for i in range(STATIONS):
        weight_cross(core, i).wait_send()
    for j in range(CHUNKS):
        source_cross_a(j).wait_send()
        for side in (0, 1):
            for p in range(PIECES):
                halo_copy(j, side, p).wait_send()
            source_halo(j, side).wait_send()
        cross_y(j).wait_send()

        @pl.when(jnp.logical_not(last_chip))
        def _():
            for p in range(PIECES):
                main_copy(j, p).wait_send()

    for d in range(1, ny):
        y_copy(d).wait_send()
    for d in range(1, nz):
        z_copy(d).wait_send()

    row = lax.broadcasted_iota(jnp.int32, (K, 128), 0)
    scaled = jnp.concatenate([acc, pltpu.roll(acc, 80, 1), pltpu.roll(acc, 112, 1)], axis=0) * (1.0 / count)
    upper = jnp.where(jnp.logical_and(lane < K, lane >= row), scaled, 0.0)
    lower = jnp.concatenate([upper, jnp.zeros((128 - K, 128), F32)], axis=0).T[:K]
    w = jnp.where(lane > row, upper, lower) + jnp.where(lane == row + 64, 1.0, 0.0)
    for start in range(0, K, BLOCK):
        columns = [jnp.broadcast_to(w[:, start + b:start + b + 1], (K, 128)) for b in range(BLOCK)]
        for b in range(BLOCK):
            j = start + b
            inverse = lax.rsqrt(columns[b][j:j + 1, :])
            unit = w[j:j + 1, :] * inverse
            column = jnp.where(row > j, columns[b] * inverse, 0.0)
            for later in range(b + 1, BLOCK):
                columns[later] = columns[later] - column * (columns[later][j:j + 1, :] * inverse)
            w = jnp.where(row == j, unit, w - column * unit)
    w_ref[...] = w


def basis_kernel(lz, yt, w_ref, o_ref, u_ref):
    rows = lz * KC
    w = w_ref[...]
    lane = lax.broadcasted_iota(jnp.int32, (K, 128), 1)
    row = lax.broadcasted_iota(jnp.int32, (K, 128), 0)
    u_ref[...] = jnp.where(lane >= row, w, 0.0)[:, :K]
    tile_row = lax.broadcasted_iota(jnp.int32, (K, lz * K), 0)
    tile_lane = lax.broadcasted_iota(jnp.int32, (K, lz * K), 1)
    copies = (tile_row == lax.rem(tile_lane, K)).astype(F32).astype(BF)
    high = w.astype(BF)
    low = (w - high.astype(F32)).astype(BF)
    block_row = lax.broadcasted_iota(jnp.int32, (rows, lz * K), 0)
    block_lane = lax.broadcasted_iota(jnp.int32, (rows, lz * K), 1)
    same = block_row // KC == block_lane // K
    out = None
    for part in (high, low):
        tiled = lax.dot_general(part, copies, (((0,), (0,)), ((), ())), preferred_element_type=F32)
        blocks = []
        for c in range(2 * CHUNKS):
            one = tiled[64 + c * KC:64 + (c + 1) * KC]
            blocks.append(jnp.where(same, jnp.concatenate([one] * lz, axis=0), 0.0))
        block = jnp.concatenate(blocks, axis=0).astype(BF)
        term = jnp.dot(yt[...], block, preferred_element_type=F32)
        out = term if out is None else out + term
    o_ref[...] = out.astype(BF)


def local(sizes, count, inverse_blocks, coupling, sources):
    ng, ny, nz = sizes
    fn = inverse_blocks.shape[1]
    lz = sources.shape[2] // K
    rows = lz * KC
    half = STATIONS * KC
    hbm = pl.BlockSpec(memory_space=pltpu.HBM)
    vmem = pl.BlockSpec(memory_space=pltpu.VMEM)
    dma = pltpu.SemaphoreType.DMA
    yt, factors = pl.pallas_call(
        functools.partial(march_kernel, sizes, lz, fn, count),
        name="march",
        out_shape=(pltpu.VMEM((fn, lz * K), BF), pltpu.VMEM((K, 128), F32)),
        in_specs=[hbm, hbm, hbm],
        out_specs=(vmem, vmem),
        scratch_shapes=[
            pltpu.VMEM((STATIONS, fn, fn), BF),
            pltpu.VMEM((STATIONS - STATIONS // 2, fn, fn), BF),
            pltpu.VMEM((2, STATIONS, fn, fn), BF),
            pltpu.VMEM((STATIONS, fn), F32),
            pltpu.VMEM((2, 2 * STATIONS, fn), F32),
            pltpu.VMEM((fn, lz * K), BF),
            pltpu.VMEM((CHUNKS, rows, fn), BF),
            pltpu.VMEM((CHUNKS, rows, fn), BF),
            pltpu.VMEM((CHUNKS, 2 * half + rows, fn), BF),
            pltpu.VMEM((CHUNKS, 3 * rows, fn), BF),
            pltpu.VMEM((CHUNKS, rows, fn), BF),
            pltpu.VMEM((3 * rows, fn), BF),
            pltpu.VMEM((3 * rows, fn), BF),
            pltpu.VMEM((2, CHUNKS, rows, fn), BF),
            pltpu.VMEM((2, CHUNKS, rows, fn), BF),
            pltpu.VMEM((ny, K // 3, 128), F32),
            pltpu.VMEM((nz, K // 3, 128), F32),
            dma((STATIONS + 2,)),
            dma((STATIONS,)), dma((STATIONS,)),
            dma((1,)), dma((1,)),
            dma((CHUNKS,)), dma((CHUNKS,)),
            dma((CHUNKS, 2)), dma((CHUNKS, 2)),
            dma((CHUNKS, PIECES)), dma((CHUNKS, PIECES)),
            dma((CHUNKS, 2, PIECES)), dma((CHUNKS, 2, PIECES)),
            dma((CHUNKS,)), dma((CHUNKS,)),
            dma((ny - 1,)), dma((ny - 1,)),
            dma((nz - 1,)), dma((nz - 1,)),
        ],
        compiler_params=pltpu.CompilerParams(collective_id=0, has_side_effects=True, vmem_limit_bytes=60 << 20),
    )(inverse_blocks, coupling, sources[0])
    basis, upper = pl.pallas_call(
        functools.partial(basis_kernel, lz),
        name="basis",
        out_shape=(jax.ShapeDtypeStruct((fn, lz * K), BF), jax.ShapeDtypeStruct((K, K), F32)),
        in_specs=[vmem, vmem],
        out_specs=(vmem, vmem),
        compiler_params=pltpu.CompilerParams(vmem_limit_bytes=32 << 20),
    )(yt, factors)
    return basis[None], upper[None]


def solution(mesh):
    placed = (P("section", None, None), P("section", None), P("section", None, "span"))
    sizes = grid_sizes(mesh)

    def whole(inverse_blocks, coupling, sources):
        count = float(sources.shape[1] * sources.shape[2] // K)
        return jax.shard_map(
            functools.partial(local, sizes, count),
            mesh=mesh,
            in_specs=placed,
            out_specs=(P("section", None, "span"), P("section", None, None)),
            check_vma=False,
        )(inverse_blocks, coupling, sources)

    return whole
```

```python
import functools

import jax
import jax.numpy as jnp
from jax import lax
from jax.experimental import pallas as pl
from jax.experimental.pallas import tpu as pltpu
from jax.sharding import PartitionSpec as P

MESH = pl.DeviceIdType.MESH
K = 48
STATIONS = 4
KC = 8
CHUNKS = 3
PIECES = 3
BLOCK = 8
BF = jnp.bfloat16
F32 = jnp.float32


def grid_sizes(mesh):
    span = mesh.shape["span"]
    rows = 4 if span == 32 else 2
    return mesh.shape["section"], rows, span // rows


def march_kernel(sizes, lz, fn, count, a_hbm, c_hbm, s_hbm, yt, w_ref,
                 av, aw, at, cv, cc, sv, tmp, sa, sb, ext, inc, wa, wb, ym, yf, gy, gz,
                 lsem, wsend, wrecv, csend, crecv, ssend, srecv, bsend, brecv,
                 msend, mrecv, hsend, hrecv, xsend, xrecv, ysend, yrecv, zsend, zrecv):
    ng, ny, nz = sizes
    ns = ny * nz
    rows = lz * KC
    half = STATIONS * KC
    g = lax.axis_index("section")
    s = lax.axis_index("span")
    core = lax.rem(g, 2)
    my, mz = s // nz, lax.rem(s, nz)
    left = (g, lax.rem(s + ns - 1, ns))
    right = (g, lax.rem(s + 1, ns))
    other = (g + 1 - 2 * core, s)
    below = (lax.rem(g + ng - 2, ng), s)
    above = (lax.rem(g + 2, ng), s)
    first_chip = g >= ng - 2
    last_chip = g < 2
    is_one = core == 1
    is_zero = core == 0

    source_copy = pltpu.make_async_copy(s_hbm, sv, lsem.at[STATIONS])
    source_copy.start()
    rate_copy = pltpu.make_async_copy(c_hbm, cv, lsem.at[STATIONS + 1])
    rate_copy.start()
    weight_copies = [pltpu.make_async_copy(a_hbm.at[i], av.at[i], lsem.at[i]) for i in range(STATIONS)]
    for i in reversed(range(STATIONS)):
        weight_copies[i].start()

    barrier = pltpu.get_barrier_semaphore()

    def greet(device):
        pl.semaphore_signal(barrier, inc=1, device_id=device, device_id_type=MESH)

    y_peer = lambda d: (g, lax.rem(my + d, ny) * nz + mz)
    z_peer = lambda d: (g, my * nz + lax.rem(mz + d, nz))
    for device in [left, right, other, below, above]:
        greet(device)
    for d in range(1, ny):
        greet(y_peer(d))
    for d in range(1, nz):
        greet(z_peer(d))

    def remote(src, dst, send, recv, device):
        return pltpu.make_async_remote_copy(
            src_ref=src, dst_ref=dst, send_sem=send, recv_sem=recv, device_id=device, device_id_type=MESH)

    early = STATIONS // 2

    def weight_cross(p, i):
        if i >= early:
            return remote(av.at[i], aw.at[i - early], wsend.at[i], wrecv.at[i], other)
        return remote(at.at[p, i], at.at[p, i], wsend.at[i], wrecv.at[i], other)

    rate_cross = lambda p: remote(cc.at[p], cc.at[p], csend.at[0], crecv.at[0], other)
    middle = pl.ds(half, rows)
    source_cross_a = lambda j: remote(tmp.at[j], sa.at[j], ssend.at[j], srecv.at[j], other)
    source_cross_b = lambda j: remote(tmp.at[j], sb.at[j, middle], ssend.at[j], srecv.at[j], other)
    width = fn // PIECES
    lanes = lambda p: pl.ds(p * width, width)
    everything = pl.ds(0, rows)

    def main_copy(j, p):
        return remote(ym.at[0, j, everything, lanes(p)], inc.at[j, everything, lanes(p)],
                      msend.at[j, p], mrecv.at[j, p], below)

    cross_y = lambda j: remote(ym.at[1 - core, j], yf.at[core, j], xsend.at[j], xrecv.at[j], other)

    def halo_copy(j, side, p):
        target, device = ((2 * rows, left), (0, right))[side]
        return remote(ext.at[j, pl.ds(rows, rows), lanes(p)], ext.at[j, pl.ds(target, rows), lanes(p)],
                      hsend.at[j, side, p], hrecv.at[j, side, p], device)

    def source_halo(j, side):
        start, target, device = ((half, half + rows, left), (rows, 0, right))[side]
        return remote(sb.at[j, pl.ds(start, half)], sb.at[j, pl.ds(target, half)],
                      bsend.at[j, side], brecv.at[j, side], device)

    source_copy.wait()
    total = 2 * CHUNKS * rows
    pick_row = lax.broadcasted_iota(jnp.int32, (CHUNKS * rows, lz * K), 0)
    pick_lane = lax.broadcasted_iota(jnp.int32, (CHUNKS * rows, lz * K), 1)
    in_chunk = lax.rem(pick_row, rows)
    source_lane = (in_chunk // KC) * K + (pick_row // rows) * KC + lax.rem(in_chunk, KC)

    def columns(h):
        pick = (pick_lane == source_lane + h * (K // 2)).astype(F32).astype(BF)
        moved = lax.dot_general(pick, sv[...], (((1,), (1,)), ((), ())), preferred_element_type=F32)
        return moved.astype(BF).reshape(CHUNKS, rows, fn)

    tmp[...] = columns(1 - core)
    pl.semaphore_wait(barrier, ny + nz + 3)

    for j in range(CHUNKS):
        @pl.when(is_one)
        def _():
            source_cross_a(j).start()

        @pl.when(is_zero)
        def _():
            source_cross_b(j).start()

        if j < STATIONS - early:
            weight_copies[STATIONS - 1 - j].wait()
            weight_cross(core, STATIONS - 1 - j).start()
    mine = columns(core)

    @pl.when(is_one)
    def _():
        sa[...] = mine

    @pl.when(is_zero)
    def _():
        sb[:, middle, :] = mine

    def begin(j):
        @pl.when(first_chip)
        def _():
            @pl.when(is_zero)
            def _():
                source_cross_a(j).wait_recv()

            ext[j, pl.ds(rows, rows), :] = sa[j]
            for p in range(PIECES):
                halo_copy(j, 0, p).start()
                halo_copy(j, 1, p).start()

    def share_sources(j):
        @pl.when(is_one)
        def _():
            source_cross_b(j).wait_recv()

        @pl.when(jnp.logical_and(is_zero, jnp.logical_not(first_chip)))
        def _():
            source_cross_a(j).wait_recv()

        source_halo(j, 0).start()
        source_halo(j, 1).start()

    begin(0)
    share_sources(0)
    rate_copy.wait()
    cc[core] = jnp.concatenate([cv[...], jnp.zeros_like(cv)], axis=0)
    rate_cross(core).start()
    for i in reversed(range(STATIONS)):
        if i < early:
            weight_copies[i].wait()
        at[core, i] = av[i].T
        if i < early:
            weight_cross(core, i).start()
        if i == early:
            begin(1)
            share_sources(1)
    begin(2)
    share_sources(2)

    rate_cross(1 - core).wait_recv()

    for i in reversed(range(early, STATIONS)):
        weight_cross(1 - core, i).wait_recv()
        at[1 - core, i] = aw[i - early].T

    @pl.when(jnp.logical_not(first_chip))
    def _():
        for i in reversed(range(early)):
            weight_cross(1 - core, i).wait_recv()

    def prepare(j):
        @pl.when(jnp.logical_not(first_chip))
        def _():
            for p in range(PIECES):
                main_copy(j, p).wait_recv()
                at_piece = (j, everything, lanes(p))
                ext[j, pl.ds(rows, rows), lanes(p)] = (inc[at_piece].astype(F32) + sa[at_piece].astype(F32)).astype(BF)
                halo_copy(j, 0, p).start()
                halo_copy(j, 1, p).start()

    def arrive(first, p, i):
        if first and i < early:
            @pl.when(jnp.logical_and(first_chip, core != p))
            def _():
                weight_cross(p, i).wait_recv()

    def spread_out(value, rates):
        w = value.astype(F32)
        center = w[KC:-KC]
        spread = w[2 * KC:] + w[:-2 * KC] - 2.0 * center
        return (center + rates * spread).astype(BF)

    def diffuse(first, p, i, value):
        arrive(first, p, i)
        return spread_out(value, cc[p, i:i + 1, :])

    def station(first, p, i, value):
        return jnp.dot(diffuse(first, p, i, value), at[p, i], preferred_element_type=F32).astype(BF)

    def compute(j, first):
        n = 3 * rows
        step = 2 * KC
        product = None
        for p in range(PIECES):
            halo_copy(j, 0, p).wait_recv()
            halo_copy(j, 1, p).wait_recv()
            update = spread_out(ext[j, :, lanes(p)], cc[1, 3:4, lanes(p)])
            term = jnp.dot(update, at[1, 3, lanes(p), :], preferred_element_type=F32)
            product = term if product is None else product + term
        wa[pl.ds(0, n - step), :] = product.astype(BF)
        wb[pl.ds(0, n - 2 * step), :] = station(first, 1, 2, wa[pl.ds(0, n - step), :])
        wa[pl.ds(0, n - 3 * step), :] = station(first, 1, 1, wb[pl.ds(0, n - 2 * step), :])
        n = 2 * rows
        upper_out = station(first, 1, 0, wa[pl.ds(0, n + step), :])
        wb[pl.ds(0, n), :] = upper_out
        ym[1, j] = wb[middle, :]

        @pl.when(is_zero)
        def _():
            cross_y(j).start()

        source_halo(j, 0).wait_recv()
        source_halo(j, 1).wait_recv()
        value = (upper_out.astype(F32) + sb[j].astype(F32)).astype(BF)
        wa[pl.ds(0, n - step), :] = station(first, 0, 3, value)
        wb[pl.ds(0, n - 2 * step), :] = station(first, 0, 2, wa[pl.ds(0, n - step), :])

        wa[pl.ds(0, n - 3 * step), :] = station(first, 0, 1, wb[pl.ds(0, n - 2 * step), :])
        if first:
            prepare(2)
        update = diffuse(first, 0, 0, wa[pl.ds(0, n - 3 * step), :])
        for p in range(PIECES):
            ym[0, j, everything, lanes(p)] = jnp.dot(
                update, at[0, 0, :, lanes(p)], preferred_element_type=F32).astype(BF)

            @pl.when(jnp.logical_not(last_chip))
            def _():
                main_copy(j, p).start()

        yf[core, j] = ym[core, j]

        @pl.when(is_one)
        def _():
            cross_y(j).start()

    prepare(0)
    prepare(1)

    compute(0, True)

    def chunk_step(j, carry):
        compute(j, False)
        return carry

    lax.fori_loop(1, CHUNKS, chunk_step, 0)
    for j in range(CHUNKS):
        cross_y(j).wait_recv()

    flat = yf[...].reshape(total, fn)
    gram = lax.dot_general(flat, flat, (((1,), (1,)), ((), ())), preferred_element_type=F32)
    group = (lax.broadcasted_iota(jnp.int32, (KC, total), 1) & (rows - 1)) // KC
    parts = []
    for c in range(2 * CHUNKS):
        part = None
        for z in range(lz):
            first = c * rows + z * KC
            one = jnp.where(group == z, gram[first:first + KC], 0.0)
            part = one if part is None else part + one
        parts.append(part)
    gram = jnp.concatenate(parts, axis=0)
    lane = lax.broadcasted_iota(jnp.int32, (K, 128), 1)
    packed = jnp.zeros((K, 128), F32)
    for pair in range(CHUNKS):
        tile = gram[:, pair * 128:(pair + 1) * 128]
        for shift in (32, 16, 8):
            tile = tile + pltpu.roll(tile, shift, 1)
        for c in (2 * pair, 2 * pair + 1):
            end = (c % 2) * rows + rows - KC
            moved = pltpu.roll(tile, (c * KC - end) % 128, 1)
            packed = jnp.where(lane // KC == c, moved, packed)
    first, second, third = packed[:16], packed[16:32], packed[32:]
    top = lax.broadcasted_iota(jnp.int32, (16, 128), 1)
    sides = jnp.where(top < 64, pltpu.roll(third, 16, 1), pltpu.roll(second, 48, 1))
    gy[my] = jnp.where(top < K, first, jnp.where(top < 96, sides, 0.0))

    y_copy = lambda d: remote(gy.at[my], gy.at[my], ysend.at[d - 1], yrecv.at[d - 1], y_peer(d))
    z_copy = lambda d: remote(gz.at[mz], gz.at[mz], zsend.at[d - 1], zrecv.at[d - 1], z_peer(d))

    for d in sorted(range(1, ny), key=lambda d: -min(d, ny - d)):
        y_copy(d).start()
    yt[...] = flat.T
    for d in range(1, ny):
        y_copy(d).wait_recv()
    acc = gy[0]
    for i in range(1, ny):
        acc = acc + gy[i]
    gz[mz] = acc
    for d in sorted(range(1, nz), key=lambda d: -min(d, nz - d)):
        z_copy(d).start()
    for d in range(1, nz):
        z_copy(d).wait_recv()
    acc = gz[0]
    for i in range(1, nz):
        acc = acc + gz[i]

    rate_cross(core).wait_send()
    for i in range(STATIONS):
        weight_cross(core, i).wait_send()
    for j in range(CHUNKS):
        source_cross_a(j).wait_send()
        for side in (0, 1):
            for p in range(PIECES):
                halo_copy(j, side, p).wait_send()
            source_halo(j, side).wait_send()
        cross_y(j).wait_send()

        @pl.when(jnp.logical_not(last_chip))
        def _():
            for p in range(PIECES):
                main_copy(j, p).wait_send()

    for d in range(1, ny):
        y_copy(d).wait_send()
    for d in range(1, nz):
        z_copy(d).wait_send()

    row = lax.broadcasted_iota(jnp.int32, (K, 128), 0)
    scaled = jnp.concatenate([acc, pltpu.roll(acc, 80, 1), pltpu.roll(acc, 112, 1)], axis=0) * (1.0 / count)
    upper = jnp.where(jnp.logical_and(lane < K, lane >= row), scaled, 0.0)
    lower = jnp.concatenate([upper, jnp.zeros((128 - K, 128), F32)], axis=0).T[:K]
    w = jnp.where(lane > row, upper, lower) + jnp.where(lane == row + 64, 1.0, 0.0)
    for start in range(0, K, BLOCK):
        columns = [jnp.broadcast_to(w[:, start + b:start + b + 1], (K, 128)) for b in range(BLOCK)]
        for b in range(BLOCK):
            j = start + b
            inverse = lax.rsqrt(columns[b][j:j + 1, :])
            unit = w[j:j + 1, :] * inverse
            column = jnp.where(row > j, columns[b] * inverse, 0.0)
            for later in range(b + 1, BLOCK):
                columns[later] = columns[later] - column * (columns[later][j:j + 1, :] * inverse)
            w = jnp.where(row == j, unit, w - column * unit)
    w_ref[...] = w


def basis_kernel(lz, yt, w_ref, o_ref, u_ref):
    rows = lz * KC
    w = w_ref[...]
    lane = lax.broadcasted_iota(jnp.int32, (K, 128), 1)
    row = lax.broadcasted_iota(jnp.int32, (K, 128), 0)
    u_ref[...] = jnp.where(lane >= row, w, 0.0)[:, :K]
    tile_row = lax.broadcasted_iota(jnp.int32, (K, lz * K), 0)
    tile_lane = lax.broadcasted_iota(jnp.int32, (K, lz * K), 1)
    copies = (tile_row == lax.rem(tile_lane, K)).astype(F32).astype(BF)
    high = w.astype(BF)
    low = (w - high.astype(F32)).astype(BF)
    block_row = lax.broadcasted_iota(jnp.int32, (rows, lz * K), 0)
    block_lane = lax.broadcasted_iota(jnp.int32, (rows, lz * K), 1)
    same = block_row // KC == block_lane // K
    blocks = []
    for part in (high, low):
        tiled = lax.dot_general(part, copies, (((0,), (0,)), ((), ())), preferred_element_type=F32)
        for c in range(2 * CHUNKS):
            one = tiled[64 + c * KC:64 + (c + 1) * KC]
            blocks.append(jnp.where(same, jnp.concatenate([one] * lz, axis=0), 0.0))
    block = jnp.concatenate(blocks, axis=0).astype(BF)
    twice = jnp.concatenate([yt[...], yt[...]], axis=1)
    o_ref[...] = jnp.dot(twice, block, preferred_element_type=F32).astype(BF)


def local(sizes, count, inverse_blocks, coupling, sources):
    ng, ny, nz = sizes
    fn = inverse_blocks.shape[1]
    lz = sources.shape[2] // K
    rows = lz * KC
    half = STATIONS * KC
    hbm = pl.BlockSpec(memory_space=pltpu.HBM)
    vmem = pl.BlockSpec(memory_space=pltpu.VMEM)
    dma = pltpu.SemaphoreType.DMA
    yt, factors = pl.pallas_call(
        functools.partial(march_kernel, sizes, lz, fn, count),
        name="march",
        out_shape=(pltpu.VMEM((fn, lz * K), BF), pltpu.VMEM((K, 128), F32)),
        in_specs=[hbm, hbm, hbm],
        out_specs=(vmem, vmem),
        scratch_shapes=[
            pltpu.VMEM((STATIONS, fn, fn), BF),
            pltpu.VMEM((STATIONS - STATIONS // 2, fn, fn), BF),
            pltpu.VMEM((2, STATIONS, fn, fn), BF),
            pltpu.VMEM((STATIONS, fn), F32),
            pltpu.VMEM((2, 2 * STATIONS, fn), F32),
            pltpu.VMEM((fn, lz * K), BF),
            pltpu.VMEM((CHUNKS, rows, fn), BF),
            pltpu.VMEM((CHUNKS, rows, fn), BF),
            pltpu.VMEM((CHUNKS, 2 * half + rows, fn), BF),
            pltpu.VMEM((CHUNKS, 3 * rows, fn), BF),
            pltpu.VMEM((CHUNKS, rows, fn), BF),
            pltpu.VMEM((3 * rows, fn), BF),
            pltpu.VMEM((3 * rows, fn), BF),
            pltpu.VMEM((2, CHUNKS, rows, fn), BF),
            pltpu.VMEM((2, CHUNKS, rows, fn), BF),
            pltpu.VMEM((ny, K // 3, 128), F32),
            pltpu.VMEM((nz, K // 3, 128), F32),
            dma((STATIONS + 2,)),
            dma((STATIONS,)), dma((STATIONS,)),
            dma((1,)), dma((1,)),
            dma((CHUNKS,)), dma((CHUNKS,)),
            dma((CHUNKS, 2)), dma((CHUNKS, 2)),
            dma((CHUNKS, PIECES)), dma((CHUNKS, PIECES)),
            dma((CHUNKS, 2, PIECES)), dma((CHUNKS, 2, PIECES)),
            dma((CHUNKS,)), dma((CHUNKS,)),
            dma((ny - 1,)), dma((ny - 1,)),
            dma((nz - 1,)), dma((nz - 1,)),
        ],
        compiler_params=pltpu.CompilerParams(collective_id=0, has_side_effects=True, vmem_limit_bytes=60 << 20),
    )(inverse_blocks, coupling, sources[0])
    basis, upper = pl.pallas_call(
        functools.partial(basis_kernel, lz),
        name="basis",
        out_shape=(jax.ShapeDtypeStruct((fn, lz * K), BF), jax.ShapeDtypeStruct((K, K), F32)),
        in_specs=[vmem, vmem],
        out_specs=(vmem, vmem),
        compiler_params=pltpu.CompilerParams(vmem_limit_bytes=32 << 20),
    )(yt, factors)
    return basis[None], upper[None]


def solution(mesh):
    placed = (P("section", None, None), P("section", None), P("section", None, "span"))
    sizes = grid_sizes(mesh)

    def whole(inverse_blocks, coupling, sources):
        count = float(sources.shape[1] * sources.shape[2] // K)
        return jax.shard_map(
            functools.partial(local, sizes, count),
            mesh=mesh,
            in_specs=placed,
            out_specs=(P("section", None, "span"), P("section", None, None)),
            check_vma=False,
        )(inverse_blocks, coupling, sources)

    return whole
```

```python
import functools

import jax
import jax.numpy as jnp
from jax import lax
from jax.experimental import pallas as pl
from jax.experimental.pallas import tpu as pltpu
from jax.sharding import PartitionSpec as P

MESH = pl.DeviceIdType.MESH
K = 48
STATIONS = 4
KC = 8
CHUNKS = 3
PIECES = 3
BLOCK = 8
BF = jnp.bfloat16
F32 = jnp.float32


def grid_sizes(mesh):
    span = mesh.shape["span"]
    rows = 4 if span == 32 else 2
    return mesh.shape["section"], rows, span // rows


def march_kernel(sizes, lz, fn, count, a_hbm, c_hbm, s_hbm, yt, w_ref,
                 av, aw, at, cv, cc, sv, tmp, sa, sb, ext, inc, wa, wb, ym, yf, gy, gz,
                 lsem, wsend, wrecv, csend, crecv, ssend, srecv, bsend, brecv,
                 msend, mrecv, hsend, hrecv, xsend, xrecv, ysend, yrecv, zsend, zrecv):
    ng, ny, nz = sizes
    ns = ny * nz
    rows = lz * KC
    half = STATIONS * KC
    g = lax.axis_index("section")
    s = lax.axis_index("span")
    core = lax.rem(g, 2)
    my, mz = s // nz, lax.rem(s, nz)
    left = (g, lax.rem(s + ns - 1, ns))
    right = (g, lax.rem(s + 1, ns))
    other = (g + 1 - 2 * core, s)
    below = (lax.rem(g + ng - 2, ng), s)
    above = (lax.rem(g + 2, ng), s)
    first_chip = g >= ng - 2
    last_chip = g < 2
    is_one = core == 1
    is_zero = core == 0

    source_copy = pltpu.make_async_copy(s_hbm, sv, lsem.at[STATIONS])
    source_copy.start()
    rate_copy = pltpu.make_async_copy(c_hbm, cv, lsem.at[STATIONS + 1])
    rate_copy.start()
    weight_copies = [pltpu.make_async_copy(a_hbm.at[i], av.at[i], lsem.at[i]) for i in range(STATIONS)]
    for i in reversed(range(STATIONS)):
        weight_copies[i].start()

    barrier = pltpu.get_barrier_semaphore()

    def greet(device):
        pl.semaphore_signal(barrier, inc=1, device_id=device, device_id_type=MESH)

    y_peer = lambda d: (g, lax.rem(my + d, ny) * nz + mz)
    z_peer = lambda d: (g, my * nz + lax.rem(mz + d, nz))
    for device in [left, right, other, below, above]:
        greet(device)
    for d in range(1, ny):
        greet(y_peer(d))
    for d in range(1, nz):
        greet(z_peer(d))

    def remote(src, dst, send, recv, device):
        return pltpu.make_async_remote_copy(
            src_ref=src, dst_ref=dst, send_sem=send, recv_sem=recv, device_id=device, device_id_type=MESH)

    early = STATIONS // 2

    def weight_cross(p, i):
        if i >= early:
            return remote(av.at[i], aw.at[i - early], wsend.at[i], wrecv.at[i], other)
        return remote(at.at[p, i], at.at[p, i], wsend.at[i], wrecv.at[i], other)

    rate_cross = lambda p: remote(cc.at[p], cc.at[p], csend.at[0], crecv.at[0], other)
    middle = pl.ds(half, rows)
    source_cross_a = lambda j: remote(tmp.at[j], sa.at[j], ssend.at[j], srecv.at[j], other)
    source_cross_b = lambda j: remote(tmp.at[j], sb.at[j, middle], ssend.at[j], srecv.at[j], other)
    width = fn // PIECES
    lanes = lambda p: pl.ds(p * width, width)
    everything = pl.ds(0, rows)

    def main_copy(j, p):
        return remote(ym.at[0, j, everything, lanes(p)], inc.at[j, everything, lanes(p)],
                      msend.at[j, p], mrecv.at[j, p], below)

    cross_y = lambda j: remote(ym.at[1 - core, j], yf.at[core, j], xsend.at[j], xrecv.at[j], other)

    def halo_copy(j, side, p):
        target, device = ((2 * rows, left), (0, right))[side]
        return remote(ext.at[j, pl.ds(rows, rows), lanes(p)], ext.at[j, pl.ds(target, rows), lanes(p)],
                      hsend.at[j, side, p], hrecv.at[j, side, p], device)

    def source_halo(j, side):
        start, target, device = ((half, half + rows, left), (rows, 0, right))[side]
        return remote(sb.at[j, pl.ds(start, half)], sb.at[j, pl.ds(target, half)],
                      bsend.at[j, side], brecv.at[j, side], device)

    total = 2 * CHUNKS * rows
    pick_row = lax.broadcasted_iota(jnp.int32, (CHUNKS * rows, lz * K), 0)
    pick_lane = lax.broadcasted_iota(jnp.int32, (CHUNKS * rows, lz * K), 1)
    in_chunk = lax.rem(pick_row, rows)
    source_lane = (in_chunk // KC) * K + (pick_row // rows) * KC + lax.rem(in_chunk, KC)

    def selection(h):
        return (pick_lane == source_lane + h * (K // 2)).astype(F32).astype(BF)

    def columns(pick):
        moved = lax.dot_general(pick, sv[...], (((1,), (1,)), ((), ())), preferred_element_type=F32)
        return moved.astype(BF).reshape(CHUNKS, rows, fn)

    pick_theirs, pick_mine = selection(1 - core), selection(core)
    source_copy.wait()
    tmp[...] = columns(pick_theirs)
    pl.semaphore_wait(barrier, ny + nz + 3)

    for j in range(CHUNKS):
        @pl.when(is_one)
        def _():
            source_cross_a(j).start()

        @pl.when(is_zero)
        def _():
            source_cross_b(j).start()

        if j < STATIONS - early:
            weight_copies[STATIONS - 1 - j].wait()
            weight_cross(core, STATIONS - 1 - j).start()
    mine = columns(pick_mine)

    @pl.when(is_one)
    def _():
        sa[...] = mine

    @pl.when(is_zero)
    def _():
        sb[:, middle, :] = mine

    def begin(j):
        @pl.when(first_chip)
        def _():
            @pl.when(is_zero)
            def _():
                source_cross_a(j).wait_recv()

            ext[j, pl.ds(rows, rows), :] = sa[j]
            for p in range(PIECES):
                halo_copy(j, 0, p).start()
                halo_copy(j, 1, p).start()

    def share_sources(j):
        @pl.when(is_one)
        def _():
            source_cross_b(j).wait_recv()

        @pl.when(jnp.logical_and(is_zero, jnp.logical_not(first_chip)))
        def _():
            source_cross_a(j).wait_recv()

        source_halo(j, 0).start()
        source_halo(j, 1).start()

    begin(0)
    share_sources(0)
    rate_copy.wait()
    cc[core] = jnp.concatenate([cv[...], jnp.zeros_like(cv)], axis=0)
    rate_cross(core).start()
    for i in reversed(range(STATIONS)):
        if i < early:
            weight_copies[i].wait()
        at[core, i] = av[i].T
        if i < early:
            weight_cross(core, i).start()
        if i == early:
            begin(1)
            share_sources(1)
    begin(2)
    share_sources(2)

    rate_cross(1 - core).wait_recv()

    for i in reversed(range(early, STATIONS)):
        weight_cross(1 - core, i).wait_recv()
        at[1 - core, i] = aw[i - early].T

    @pl.when(jnp.logical_not(first_chip))
    def _():
        for i in reversed(range(early)):
            weight_cross(1 - core, i).wait_recv()

    def prepare(j):
        @pl.when(jnp.logical_not(first_chip))
        def _():
            for p in range(PIECES):
                main_copy(j, p).wait_recv()
                at_piece = (j, everything, lanes(p))
                ext[j, pl.ds(rows, rows), lanes(p)] = (inc[at_piece].astype(F32) + sa[at_piece].astype(F32)).astype(BF)
                halo_copy(j, 0, p).start()
                halo_copy(j, 1, p).start()

    def arrive(first, p, i):
        if first and i < early:
            @pl.when(jnp.logical_and(first_chip, core != p))
            def _():
                weight_cross(p, i).wait_recv()

    def spread_out(value, rates):
        w = value.astype(F32)
        center = w[KC:-KC]
        spread = w[2 * KC:] + w[:-2 * KC] - 2.0 * center
        return (center + rates * spread).astype(BF)

    def diffuse(first, p, i, value):
        arrive(first, p, i)
        return spread_out(value, cc[p, i:i + 1, :])

    def station(first, p, i, value):
        return jnp.dot(diffuse(first, p, i, value), at[p, i], preferred_element_type=F32).astype(BF)

    def compute(j, first):
        n = 3 * rows
        step = 2 * KC
        product = None
        for p in range(PIECES):
            halo_copy(j, 0, p).wait_recv()
            halo_copy(j, 1, p).wait_recv()
            update = spread_out(ext[j, :, lanes(p)], cc[1, 3:4, lanes(p)])
            term = jnp.dot(update, at[1, 3, lanes(p), :], preferred_element_type=F32)
            product = term if product is None else product + term
        wa[pl.ds(0, n - step), :] = product.astype(BF)
        wb[pl.ds(0, n - 2 * step), :] = station(first, 1, 2, wa[pl.ds(0, n - step), :])
        wa[pl.ds(0, n - 3 * step), :] = station(first, 1, 1, wb[pl.ds(0, n - 2 * step), :])
        n = 2 * rows
        upper_out = station(first, 1, 0, wa[pl.ds(0, n + step), :])
        wb[pl.ds(0, n), :] = upper_out
        ym[1, j] = wb[middle, :]

        @pl.when(is_zero)
        def _():
            cross_y(j).start()

        source_halo(j, 0).wait_recv()
        source_halo(j, 1).wait_recv()
        value = (upper_out.astype(F32) + sb[j].astype(F32)).astype(BF)
        wa[pl.ds(0, n - step), :] = station(first, 0, 3, value)
        wb[pl.ds(0, n - 2 * step), :] = station(first, 0, 2, wa[pl.ds(0, n - step), :])

        wa[pl.ds(0, n - 3 * step), :] = station(first, 0, 1, wb[pl.ds(0, n - 2 * step), :])
        if first:
            prepare(2)
        update = diffuse(first, 0, 0, wa[pl.ds(0, n - 3 * step), :])
        for p in range(PIECES):
            ym[0, j, everything, lanes(p)] = jnp.dot(
                update, at[0, 0, :, lanes(p)], preferred_element_type=F32).astype(BF)

            @pl.when(jnp.logical_not(last_chip))
            def _():
                main_copy(j, p).start()

        yf[core, j] = ym[core, j]

        @pl.when(is_one)
        def _():
            cross_y(j).start()

    prepare(0)
    prepare(1)

    compute(0, True)

    def chunk_step(j, carry):
        compute(j, False)
        return carry

    lax.fori_loop(1, CHUNKS, chunk_step, 0)
    for j in range(CHUNKS):
        cross_y(j).wait_recv()

    flat = yf[...].reshape(total, fn)
    gram = lax.dot_general(flat, flat, (((1,), (1,)), ((), ())), preferred_element_type=F32)
    group = (lax.broadcasted_iota(jnp.int32, (KC, total), 1) & (rows - 1)) // KC
    parts = []
    for c in range(2 * CHUNKS):
        part = None
        for z in range(lz):
            first = c * rows + z * KC
            one = jnp.where(group == z, gram[first:first + KC], 0.0)
            part = one if part is None else part + one
        parts.append(part)
    gram = jnp.concatenate(parts, axis=0)
    lane = lax.broadcasted_iota(jnp.int32, (K, 128), 1)
    packed = jnp.zeros((K, 128), F32)
    for pair in range(CHUNKS):
        tile = gram[:, pair * 128:(pair + 1) * 128]
        for shift in (32, 16, 8):
            tile = tile + pltpu.roll(tile, shift, 1)
        for c in (2 * pair, 2 * pair + 1):
            end = (c % 2) * rows + rows - KC
            moved = pltpu.roll(tile, (c * KC - end) % 128, 1)
            packed = jnp.where(lane // KC == c, moved, packed)
    first, second, third = packed[:16], packed[16:32], packed[32:]
    top = lax.broadcasted_iota(jnp.int32, (16, 128), 1)
    sides = jnp.where(top < 64, pltpu.roll(third, 16, 1), pltpu.roll(second, 48, 1))
    gy[my] = jnp.where(top < K, first, jnp.where(top < 96, sides, 0.0))

    y_copy = lambda d: remote(gy.at[my], gy.at[my], ysend.at[d - 1], yrecv.at[d - 1], y_peer(d))
    z_copy = lambda d: remote(gz.at[mz], gz.at[mz], zsend.at[d - 1], zrecv.at[d - 1], z_peer(d))

    for d in sorted(range(1, ny), key=lambda d: -min(d, ny - d)):
        y_copy(d).start()
    yt[...] = flat.T
    for d in range(1, ny):
        y_copy(d).wait_recv()
    acc = gy[0]
    for i in range(1, ny):
        acc = acc + gy[i]
    gz[mz] = acc
    for d in sorted(range(1, nz), key=lambda d: -min(d, nz - d)):
        z_copy(d).start()
    for d in range(1, nz):
        z_copy(d).wait_recv()
    acc = gz[0]
    for i in range(1, nz):
        acc = acc + gz[i]

    rate_cross(core).wait_send()
    for i in range(STATIONS):
        weight_cross(core, i).wait_send()
    for j in range(CHUNKS):
        source_cross_a(j).wait_send()
        for side in (0, 1):
            for p in range(PIECES):
                halo_copy(j, side, p).wait_send()
            source_halo(j, side).wait_send()
        cross_y(j).wait_send()

        @pl.when(jnp.logical_not(last_chip))
        def _():
            for p in range(PIECES):
                main_copy(j, p).wait_send()

    for d in range(1, ny):
        y_copy(d).wait_send()
    for d in range(1, nz):
        z_copy(d).wait_send()

    row = lax.broadcasted_iota(jnp.int32, (K, 128), 0)
    scaled = jnp.concatenate([acc, pltpu.roll(acc, 80, 1), pltpu.roll(acc, 112, 1)], axis=0) * (1.0 / count)
    upper = jnp.where(jnp.logical_and(lane < K, lane >= row), scaled, 0.0)
    lower = jnp.concatenate([upper, jnp.zeros((128 - K, 128), F32)], axis=0).T[:K]
    w = jnp.where(lane > row, upper, lower) + jnp.where(lane == row + 64, 1.0, 0.0)
    for start in range(0, K, BLOCK):
        columns = [jnp.broadcast_to(w[:, start + b:start + b + 1], (K, 128)) for b in range(BLOCK)]
        for b in range(BLOCK):
            j = start + b
            inverse = lax.rsqrt(columns[b][j:j + 1, :])
            unit = w[j:j + 1, :] * inverse
            column = jnp.where(row > j, columns[b] * inverse, 0.0)
            for later in range(b + 1, BLOCK):
                columns[later] = columns[later] - column * (columns[later][j:j + 1, :] * inverse)
            w = jnp.where(row == j, unit, w - column * unit)
    w_ref[...] = w


def basis_kernel(lz, yt, w_ref, o_ref, u_ref):
    rows = lz * KC
    w = w_ref[...]
    lane = lax.broadcasted_iota(jnp.int32, (K, 128), 1)
    row = lax.broadcasted_iota(jnp.int32, (K, 128), 0)
    u_ref[...] = jnp.where(lane >= row, w, 0.0)[:, :K]
    tile_row = lax.broadcasted_iota(jnp.int32, (K, lz * K), 0)
    tile_lane = lax.broadcasted_iota(jnp.int32, (K, lz * K), 1)
    copies = (tile_row == lax.rem(tile_lane, K)).astype(F32).astype(BF)
    high = w.astype(BF)
    low = (w - high.astype(F32)).astype(BF)
    block_row = lax.broadcasted_iota(jnp.int32, (rows, lz * K), 0)
    block_lane = lax.broadcasted_iota(jnp.int32, (rows, lz * K), 1)
    same = block_row // KC == block_lane // K
    blocks = []
    for part in (high, low):
        tiled = lax.dot_general(part, copies, (((0,), (0,)), ((), ())), preferred_element_type=F32)
        for c in range(2 * CHUNKS):
            one = tiled[64 + c * KC:64 + (c + 1) * KC]
            blocks.append(jnp.where(same, jnp.concatenate([one] * lz, axis=0), 0.0))
    block = jnp.concatenate(blocks, axis=0).astype(BF)
    twice = jnp.concatenate([yt[...], yt[...]], axis=1)
    o_ref[...] = jnp.dot(twice, block, preferred_element_type=F32).astype(BF)


def local(sizes, count, inverse_blocks, coupling, sources):
    ng, ny, nz = sizes
    fn = inverse_blocks.shape[1]
    lz = sources.shape[2] // K
    rows = lz * KC
    half = STATIONS * KC
    hbm = pl.BlockSpec(memory_space=pltpu.HBM)
    vmem = pl.BlockSpec(memory_space=pltpu.VMEM)
    dma = pltpu.SemaphoreType.DMA
    yt, factors = pl.pallas_call(
        functools.partial(march_kernel, sizes, lz, fn, count),
        name="march",
        out_shape=(pltpu.VMEM((fn, lz * K), BF), pltpu.VMEM((K, 128), F32)),
        in_specs=[hbm, hbm, hbm],
        out_specs=(vmem, vmem),
        scratch_shapes=[
            pltpu.VMEM((STATIONS, fn, fn), BF),
            pltpu.VMEM((STATIONS - STATIONS // 2, fn, fn), BF),
            pltpu.VMEM((2, STATIONS, fn, fn), BF),
            pltpu.VMEM((STATIONS, fn), F32),
            pltpu.VMEM((2, 2 * STATIONS, fn), F32),
            pltpu.VMEM((fn, lz * K), BF),
            pltpu.VMEM((CHUNKS, rows, fn), BF),
            pltpu.VMEM((CHUNKS, rows, fn), BF),
            pltpu.VMEM((CHUNKS, 2 * half + rows, fn), BF),
            pltpu.VMEM((CHUNKS, 3 * rows, fn), BF),
            pltpu.VMEM((CHUNKS, rows, fn), BF),
            pltpu.VMEM((3 * rows, fn), BF),
            pltpu.VMEM((3 * rows, fn), BF),
            pltpu.VMEM((2, CHUNKS, rows, fn), BF),
            pltpu.VMEM((2, CHUNKS, rows, fn), BF),
            pltpu.VMEM((ny, K // 3, 128), F32),
            pltpu.VMEM((nz, K // 3, 128), F32),
            dma((STATIONS + 2,)),
            dma((STATIONS,)), dma((STATIONS,)),
            dma((1,)), dma((1,)),
            dma((CHUNKS,)), dma((CHUNKS,)),
            dma((CHUNKS, 2)), dma((CHUNKS, 2)),
            dma((CHUNKS, PIECES)), dma((CHUNKS, PIECES)),
            dma((CHUNKS, 2, PIECES)), dma((CHUNKS, 2, PIECES)),
            dma((CHUNKS,)), dma((CHUNKS,)),
            dma((ny - 1,)), dma((ny - 1,)),
            dma((nz - 1,)), dma((nz - 1,)),
        ],
        compiler_params=pltpu.CompilerParams(collective_id=0, has_side_effects=True, vmem_limit_bytes=60 << 20),
    )(inverse_blocks, coupling, sources[0])
    basis, upper = pl.pallas_call(
        functools.partial(basis_kernel, lz),
        name="basis",
        out_shape=(jax.ShapeDtypeStruct((fn, lz * K), BF), jax.ShapeDtypeStruct((K, K), F32)),
        in_specs=[vmem, vmem],
        out_specs=(vmem, vmem),
        compiler_params=pltpu.CompilerParams(vmem_limit_bytes=32 << 20),
    )(yt, factors)
    return basis[None], upper[None]


def solution(mesh):
    placed = (P("section", None, None), P("section", None), P("section", None, "span"))
    sizes = grid_sizes(mesh)

    def whole(inverse_blocks, coupling, sources):
        count = float(sources.shape[1] * sources.shape[2] // K)
        return jax.shard_map(
            functools.partial(local, sizes, count),
            mesh=mesh,
            in_specs=placed,
            out_specs=(P("section", None, "span"), P("section", None, None)),
            check_vma=False,
        )(inverse_blocks, coupling, sources)

    return whole
```

```python
import functools

import jax
import jax.numpy as jnp
from jax import lax
from jax.experimental import pallas as pl
from jax.experimental.pallas import tpu as pltpu
from jax.sharding import PartitionSpec as P

MESH = pl.DeviceIdType.MESH
K = 48
STATIONS = 4
KC = 8
CHUNKS = 3
PIECES = 3
BLOCK = 8
BF = jnp.bfloat16
F32 = jnp.float32


def grid_sizes(mesh):
    span = mesh.shape["span"]
    rows = 4 if span == 32 else 2
    return mesh.shape["section"], rows, span // rows


def march_kernel(sizes, lz, fn, count, a_hbm, c_hbm, s_hbm, yt, w_ref,
                 av, aw, at, cv, cc, sv, tmp, sa, sb, ext, inc, wa, wb, ym, yf, gy, gz,
                 lsem, wsend, wrecv, csend, crecv, ssend, srecv, bsend, brecv,
                 msend, mrecv, hsend, hrecv, xsend, xrecv, ysend, yrecv, zsend, zrecv):
    ng, ny, nz = sizes
    ns = ny * nz
    rows = lz * KC
    half = STATIONS * KC
    g = lax.axis_index("section")
    s = lax.axis_index("span")
    core = lax.rem(g, 2)
    my, mz = s // nz, lax.rem(s, nz)
    left = (g, lax.rem(s + ns - 1, ns))
    right = (g, lax.rem(s + 1, ns))
    other = (g + 1 - 2 * core, s)
    below = (lax.rem(g + ng - 2, ng), s)
    above = (lax.rem(g + 2, ng), s)
    first_chip = g >= ng - 2
    last_chip = g < 2
    is_one = core == 1
    is_zero = core == 0

    source_copy = pltpu.make_async_copy(s_hbm, sv, lsem.at[STATIONS])
    source_copy.start()
    rate_copy = pltpu.make_async_copy(c_hbm, cv, lsem.at[STATIONS + 1])
    rate_copy.start()
    weight_copies = [pltpu.make_async_copy(a_hbm.at[i], av.at[i], lsem.at[i]) for i in range(STATIONS)]
    for i in reversed(range(STATIONS)):
        weight_copies[i].start()

    barrier = pltpu.get_barrier_semaphore()

    def greet(device):
        pl.semaphore_signal(barrier, inc=1, device_id=device, device_id_type=MESH)

    y_peer = lambda d: (g, lax.rem(my + d, ny) * nz + mz)
    z_peer = lambda d: (g, my * nz + lax.rem(mz + d, nz))
    for device in [left, right, other, below, above]:
        greet(device)
    for d in range(1, ny):
        greet(y_peer(d))
    for d in range(1, nz):
        greet(z_peer(d))

    def remote(src, dst, send, recv, device):
        return pltpu.make_async_remote_copy(
            src_ref=src, dst_ref=dst, send_sem=send, recv_sem=recv, device_id=device, device_id_type=MESH)

    early = STATIONS // 2

    def weight_cross(p, i):
        if i >= early:
            return remote(av.at[i], aw.at[i - early], wsend.at[i], wrecv.at[i], other)
        return remote(at.at[p, i], at.at[p, i], wsend.at[i], wrecv.at[i], other)

    rate_cross = lambda p: remote(cc.at[p], cc.at[p], csend.at[0], crecv.at[0], other)
    middle = pl.ds(half, rows)
    source_cross_a = lambda j: remote(tmp.at[j], sa.at[j], ssend.at[j], srecv.at[j], other)
    source_cross_b = lambda j: remote(tmp.at[j], sb.at[j, middle], ssend.at[j], srecv.at[j], other)
    width = fn // PIECES
    lanes = lambda p: pl.ds(p * width, width)
    everything = pl.ds(0, rows)

    def main_copy(j, p):
        return remote(ym.at[0, j, everything, lanes(p)], inc.at[j, everything, lanes(p)],
                      msend.at[j, p], mrecv.at[j, p], below)

    cross_y = lambda j: remote(ym.at[1 - core, j], yf.at[core, j], xsend.at[j], xrecv.at[j], other)

    def halo_copy(j, side, p):
        target, device = ((2 * rows, left), (0, right))[side]
        return remote(ext.at[j, pl.ds(rows, rows), lanes(p)], ext.at[j, pl.ds(target, rows), lanes(p)],
                      hsend.at[j, side, p], hrecv.at[j, side, p], device)

    def source_halo(j, side):
        start, target, device = ((half, half + rows, left), (rows, 0, right))[side]
        return remote(sb.at[j, pl.ds(start, half)], sb.at[j, pl.ds(target, half)],
                      bsend.at[j, side], brecv.at[j, side], device)

    source_copy.wait()
    total = 2 * CHUNKS * rows
    pick_row = lax.broadcasted_iota(jnp.int32, (CHUNKS * rows, lz * K), 0)
    pick_lane = lax.broadcasted_iota(jnp.int32, (CHUNKS * rows, lz * K), 1)
    in_chunk = lax.rem(pick_row, rows)
    source_lane = (in_chunk // KC) * K + (pick_row // rows) * KC + lax.rem(in_chunk, KC)

    def columns(h):
        pick = (pick_lane == source_lane + h * (K // 2)).astype(F32).astype(BF)
        moved = lax.dot_general(pick, sv[...], (((1,), (1,)), ((), ())), preferred_element_type=F32)
        return moved.astype(BF).reshape(CHUNKS, rows, fn)

    tmp[...] = columns(1 - core)
    pl.semaphore_wait(barrier, ny + nz + 3)

    for j in range(CHUNKS):
        @pl.when(is_one)
        def _():
            source_cross_a(j).start()

        @pl.when(is_zero)
        def _():
            source_cross_b(j).start()

        if j < STATIONS - early:
            weight_copies[STATIONS - 1 - j].wait()
            weight_cross(core, STATIONS - 1 - j).start()
    mine = columns(core)

    @pl.when(is_one)
    def _():
        sa[...] = mine

    @pl.when(is_zero)
    def _():
        sb[:, middle, :] = mine

    def begin(j):
        @pl.when(first_chip)
        def _():
            @pl.when(is_zero)
            def _():
                source_cross_a(j).wait_recv()

            ext[j, pl.ds(rows, rows), :] = sa[j]
            for p in range(PIECES):
                halo_copy(j, 0, p).start()
                halo_copy(j, 1, p).start()

    def share_sources(j):
        @pl.when(is_one)
        def _():
            source_cross_b(j).wait_recv()

        @pl.when(jnp.logical_and(is_zero, jnp.logical_not(first_chip)))
        def _():
            source_cross_a(j).wait_recv()

        source_halo(j, 0).start()
        source_halo(j, 1).start()

    begin(0)
    share_sources(0)
    rate_copy.wait()
    cc[core] = jnp.concatenate([cv[...], jnp.zeros_like(cv)], axis=0)
    rate_cross(core).start()
    for i in reversed(range(STATIONS)):
        if i < early:
            weight_copies[i].wait()
        at[core, i] = av[i].T
        if i < early:
            weight_cross(core, i).start()
        if i == early:
            begin(1)
            share_sources(1)
    begin(2)
    share_sources(2)

    rate_cross(1 - core).wait_recv()

    for i in reversed(range(early, STATIONS)):
        weight_cross(1 - core, i).wait_recv()
        at[1 - core, i] = aw[i - early].T

    @pl.when(jnp.logical_not(first_chip))
    def _():
        for i in reversed(range(early)):
            weight_cross(1 - core, i).wait_recv()

    def prepare(j):
        @pl.when(jnp.logical_not(first_chip))
        def _():
            for p in range(PIECES):
                main_copy(j, p).wait_recv()
                at_piece = (j, everything, lanes(p))
                ext[j, pl.ds(rows, rows), lanes(p)] = (inc[at_piece].astype(F32) + sa[at_piece].astype(F32)).astype(BF)
                halo_copy(j, 0, p).start()
                halo_copy(j, 1, p).start()

    def arrive(first, p, i):
        if first and i < early:
            @pl.when(jnp.logical_and(first_chip, core != p))
            def _():
                weight_cross(p, i).wait_recv()

    def spread_out(value, rates):
        w = value.astype(F32)
        center = w[KC:-KC]
        spread = w[2 * KC:] + w[:-2 * KC] - 2.0 * center
        return (center + rates * spread).astype(BF)

    def diffuse(first, p, i, value):
        arrive(first, p, i)
        return spread_out(value, cc[p, i:i + 1, :])

    def station(first, p, i, value):
        return jnp.dot(diffuse(first, p, i, value), at[p, i], preferred_element_type=F32).astype(BF)

    def compute(j, first):
        n = 3 * rows
        step = 2 * KC
        product = None
        for p in range(PIECES):
            halo_copy(j, 0, p).wait_recv()
            halo_copy(j, 1, p).wait_recv()
            update = spread_out(ext[j, :, lanes(p)], cc[1, 3:4, lanes(p)])
            term = jnp.dot(update, at[1, 3, lanes(p), :], preferred_element_type=F32)
            product = term if product is None else product + term
        wa[pl.ds(0, n - step), :] = product.astype(BF)
        wb[pl.ds(0, n - 2 * step), :] = station(first, 1, 2, wa[pl.ds(0, n - step), :])
        wa[pl.ds(0, n - 3 * step), :] = station(first, 1, 1, wb[pl.ds(0, n - 2 * step), :])
        n = 2 * rows
        upper_out = station(first, 1, 0, wa[pl.ds(0, n + step), :])
        wb[pl.ds(0, n), :] = upper_out
        ym[1, j] = wb[middle, :]

        @pl.when(is_zero)
        def _():
            cross_y(j).start()

        source_halo(j, 0).wait_recv()
        source_halo(j, 1).wait_recv()
        value = (upper_out.astype(F32) + sb[j].astype(F32)).astype(BF)
        wa[pl.ds(0, n - step), :] = station(first, 0, 3, value)
        wb[pl.ds(0, n - 2 * step), :] = station(first, 0, 2, wa[pl.ds(0, n - step), :])

        wa[pl.ds(0, n - 3 * step), :] = station(first, 0, 1, wb[pl.ds(0, n - 2 * step), :])
        if first:
            prepare(2)
        update = diffuse(first, 0, 0, wa[pl.ds(0, n - 3 * step), :])
        for p in range(PIECES):
            ym[0, j, everything, lanes(p)] = jnp.dot(
                update, at[0, 0, :, lanes(p)], preferred_element_type=F32).astype(BF)

            @pl.when(jnp.logical_not(last_chip))
            def _():
                main_copy(j, p).start()

        yf[core, j] = ym[core, j]

        @pl.when(is_one)
        def _():
            cross_y(j).start()

    prepare(0)
    prepare(1)

    compute(0, True)

    def chunk_step(j, carry):
        compute(j, False)
        return carry

    lax.fori_loop(1, CHUNKS, chunk_step, 0)
    for j in range(CHUNKS):
        cross_y(j).wait_recv()

    flat = yf[...].reshape(total, fn)
    gram = lax.dot_general(flat, flat, (((1,), (1,)), ((), ())), preferred_element_type=F32)
    group = (lax.broadcasted_iota(jnp.int32, (KC, total), 1) & (rows - 1)) // KC
    parts = []
    for c in range(2 * CHUNKS):
        part = None
        for z in range(lz):
            first = c * rows + z * KC
            one = jnp.where(group == z, gram[first:first + KC], 0.0)
            part = one if part is None else part + one
        parts.append(part)
    gram = jnp.concatenate(parts, axis=0)
    lane = lax.broadcasted_iota(jnp.int32, (K, 128), 1)
    packed = jnp.zeros((K, 128), F32)
    for pair in range(CHUNKS):
        tile = gram[:, pair * 128:(pair + 1) * 128]
        for shift in (32, 16, 8):
            tile = tile + pltpu.roll(tile, shift, 1)
        for c in (2 * pair, 2 * pair + 1):
            end = (c % 2) * rows + rows - KC
            moved = pltpu.roll(tile, (c * KC - end) % 128, 1)
            packed = jnp.where(lane // KC == c, moved, packed)
    first, second, third = packed[:16], packed[16:32], packed[32:]
    top = lax.broadcasted_iota(jnp.int32, (16, 128), 1)
    sides = jnp.where(top < 64, pltpu.roll(third, 16, 1), pltpu.roll(second, 48, 1))
    gy[my] = jnp.where(top < K, first, jnp.where(top < 96, sides, 0.0))

    y_copy = lambda d: remote(gy.at[my], gy.at[my], ysend.at[d - 1], yrecv.at[d - 1], y_peer(d))
    z_copy = lambda d: remote(gz.at[mz], gz.at[mz], zsend.at[d - 1], zrecv.at[d - 1], z_peer(d))

    for d in sorted(range(1, ny), key=lambda d: -min(d, ny - d)):
        y_copy(d).start()
    for d in range(1, ny):
        y_copy(d).wait_recv()
    acc = gy[0]
    for i in range(1, ny):
        acc = acc + gy[i]
    gz[mz] = acc
    for d in sorted(range(1, nz), key=lambda d: -min(d, nz - d)):
        z_copy(d).start()
    yt[...] = flat.T
    for d in range(1, nz):
        z_copy(d).wait_recv()
    acc = gz[0]
    for i in range(1, nz):
        acc = acc + gz[i]

    rate_cross(core).wait_send()
    for i in range(STATIONS):
        weight_cross(core, i).wait_send()
    for j in range(CHUNKS):
        source_cross_a(j).wait_send()
        for side in (0, 1):
            for p in range(PIECES):
                halo_copy(j, side, p).wait_send()
            source_halo(j, side).wait_send()
        cross_y(j).wait_send()

        @pl.when(jnp.logical_not(last_chip))
        def _():
            for p in range(PIECES):
                main_copy(j, p).wait_send()

    for d in range(1, ny):
        y_copy(d).wait_send()
    for d in range(1, nz):
        z_copy(d).wait_send()

    row = lax.broadcasted_iota(jnp.int32, (K, 128), 0)
    scaled = jnp.concatenate([acc, pltpu.roll(acc, 80, 1), pltpu.roll(acc, 112, 1)], axis=0) * (1.0 / count)
    upper = jnp.where(jnp.logical_and(lane < K, lane >= row), scaled, 0.0)
    lower = jnp.concatenate([upper, jnp.zeros((128 - K, 128), F32)], axis=0).T[:K]
    w = jnp.where(lane > row, upper, lower) + jnp.where(lane == row + 64, 1.0, 0.0)
    for start in range(0, K, BLOCK):
        columns = [jnp.broadcast_to(w[:, start + b:start + b + 1], (K, 128)) for b in range(BLOCK)]
        for b in range(BLOCK):
            j = start + b
            inverse = lax.rsqrt(columns[b][j:j + 1, :])
            unit = w[j:j + 1, :] * inverse
            column = jnp.where(row > j, columns[b] * inverse, 0.0)
            for later in range(b + 1, BLOCK):
                columns[later] = columns[later] - column * (columns[later][j:j + 1, :] * inverse)
            w = jnp.where(row == j, unit, w - column * unit)
    w_ref[...] = w


def basis_kernel(lz, yt, w_ref, o_ref, u_ref):
    rows = lz * KC
    w = w_ref[...]
    lane = lax.broadcasted_iota(jnp.int32, (K, 128), 1)
    row = lax.broadcasted_iota(jnp.int32, (K, 128), 0)
    u_ref[...] = jnp.where(lane >= row, w, 0.0)[:, :K]
    tile_row = lax.broadcasted_iota(jnp.int32, (K, lz * K), 0)
    tile_lane = lax.broadcasted_iota(jnp.int32, (K, lz * K), 1)
    copies = (tile_row == lax.rem(tile_lane, K)).astype(F32).astype(BF)
    high = w.astype(BF)
    low = (w - high.astype(F32)).astype(BF)
    block_row = lax.broadcasted_iota(jnp.int32, (rows, lz * K), 0)
    block_lane = lax.broadcasted_iota(jnp.int32, (rows, lz * K), 1)
    same = block_row // KC == block_lane // K
    blocks = []
    for part in (high, low):
        tiled = lax.dot_general(part, copies, (((0,), (0,)), ((), ())), preferred_element_type=F32)
        for c in range(2 * CHUNKS):
            one = tiled[64 + c * KC:64 + (c + 1) * KC]
            blocks.append(jnp.where(same, jnp.concatenate([one] * lz, axis=0), 0.0))
    block = jnp.concatenate(blocks, axis=0).astype(BF)
    twice = jnp.concatenate([yt[...], yt[...]], axis=1)
    o_ref[...] = jnp.dot(twice, block, preferred_element_type=F32).astype(BF)


def local(sizes, count, inverse_blocks, coupling, sources):
    ng, ny, nz = sizes
    fn = inverse_blocks.shape[1]
    lz = sources.shape[2] // K
    rows = lz * KC
    half = STATIONS * KC
    hbm = pl.BlockSpec(memory_space=pltpu.HBM)
    vmem = pl.BlockSpec(memory_space=pltpu.VMEM)
    dma = pltpu.SemaphoreType.DMA
    yt, factors = pl.pallas_call(
        functools.partial(march_kernel, sizes, lz, fn, count),
        name="march",
        out_shape=(pltpu.VMEM((fn, lz * K), BF), pltpu.VMEM((K, 128), F32)),
        in_specs=[hbm, hbm, hbm],
        out_specs=(vmem, vmem),
        scratch_shapes=[
            pltpu.VMEM((STATIONS, fn, fn), BF),
            pltpu.VMEM((STATIONS - STATIONS // 2, fn, fn), BF),
            pltpu.VMEM((2, STATIONS, fn, fn), BF),
            pltpu.VMEM((STATIONS, fn), F32),
            pltpu.VMEM((2, 2 * STATIONS, fn), F32),
            pltpu.VMEM((fn, lz * K), BF),
            pltpu.VMEM((CHUNKS, rows, fn), BF),
            pltpu.VMEM((CHUNKS, rows, fn), BF),
            pltpu.VMEM((CHUNKS, 2 * half + rows, fn), BF),
            pltpu.VMEM((CHUNKS, 3 * rows, fn), BF),
            pltpu.VMEM((CHUNKS, rows, fn), BF),
            pltpu.VMEM((3 * rows, fn), BF),
            pltpu.VMEM((3 * rows, fn), BF),
            pltpu.VMEM((2, CHUNKS, rows, fn), BF),
            pltpu.VMEM((2, CHUNKS, rows, fn), BF),
            pltpu.VMEM((ny, K // 3, 128), F32),
            pltpu.VMEM((nz, K // 3, 128), F32),
            dma((STATIONS + 2,)),
            dma((STATIONS,)), dma((STATIONS,)),
            dma((1,)), dma((1,)),
            dma((CHUNKS,)), dma((CHUNKS,)),
            dma((CHUNKS, 2)), dma((CHUNKS, 2)),
            dma((CHUNKS, PIECES)), dma((CHUNKS, PIECES)),
            dma((CHUNKS, 2, PIECES)), dma((CHUNKS, 2, PIECES)),
            dma((CHUNKS,)), dma((CHUNKS,)),
            dma((ny - 1,)), dma((ny - 1,)),
            dma((nz - 1,)), dma((nz - 1,)),
        ],
        compiler_params=pltpu.CompilerParams(collective_id=0, has_side_effects=True, vmem_limit_bytes=60 << 20),
    )(inverse_blocks, coupling, sources[0])
    basis, upper = pl.pallas_call(
        functools.partial(basis_kernel, lz),
        name="basis",
        out_shape=(jax.ShapeDtypeStruct((fn, lz * K), BF), jax.ShapeDtypeStruct((K, K), F32)),
        in_specs=[vmem, vmem],
        out_specs=(vmem, vmem),
        compiler_params=pltpu.CompilerParams(vmem_limit_bytes=32 << 20),
    )(yt, factors)
    return basis[None], upper[None]


def solution(mesh):
    placed = (P("section", None, None), P("section", None), P("section", None, "span"))
    sizes = grid_sizes(mesh)

    def whole(inverse_blocks, coupling, sources):
        count = float(sources.shape[1] * sources.shape[2] // K)
        return jax.shard_map(
            functools.partial(local, sizes, count),
            mesh=mesh,
            in_specs=placed,
            out_specs=(P("section", None, "span"), P("section", None, None)),
            check_vma=False,
        )(inverse_blocks, coupling, sources)

    return whole
```
